128 devices in a mesh: areal: 16 (over x, y), layer: 8 (over z, core).
Axes of the slice: x: 4, y: 4, z: 4, core: 2. Of those that a mesh axis runs over, the one named last changes fastest.
Arguments:
- pressure: float32 [64, 4096, 256], P('layer', 'areal'), may hold values from -6 to 6
- saturations: float32 [2, 64, 4096, 256], P(None, 'layer', 'areal'), may hold values from 0.05 to 0.4
- old_saturations: float32 [2, 64, 4096, 256], P(None, 'layer', 'areal'), may hold values from 0.05 to 0.4
- permeability: float32 [64, 4096, 256], P('layer', 'areal'), may hold values from 0.05 to 5
- pore_volume: float32 [64, 4096, 256], P('layer', 'areal'), may hold values from 0.5 to 2
- perf_cell: int32 [8, 16, 16, 256], P('layer', 'areal'), may hold values from 0 to 65535
- perf_layer: int32 [8, 16, 16, 256], P('layer', 'areal'), may hold values from 0 to 7
- perf_seg: int32 [8, 16, 16, 256], P('layer', 'areal'), may hold values from 0 to 383
- perf_index: float32 [8, 16, 16, 256], P('layer', 'areal'), may hold values from 0.5 to 4
- perf_blocks: int32 [8, 16, 16], P('layer', 'areal'), may hold values from 0 to 2, as said below
- seg_parent: int32 [3072, 16], P('areal'), may hold values from 0 to 14, as said below
- seg_cond: float32 [3072, 16], P('areal'), may hold values from 10 to 100
- seg_target: float32 [3072, 16], P('areal'), may hold values from -6 to 6
Outputs:
- cell_residual: float32 [3, 64, 4096, 256], P(None, 'layer', 'areal')
- well_pressure: float32 [3072, 16], P('areal', 'layer')
The draws below stay inside these ranges and needn't reach their ends.
Inputs may be any that keep to these rules, and one draw needn't show every extreme that they name: `perf_blocks`: in every layer one owner index, drawn from the seed, has 2 live blocks from every areal index. Apart from it, each owner has 2 live blocks from its own areal index, 1 to 2 from the areal indices next to it (circularly), and 0 to 1 from the others. `seg_parent`: segment 0 has parent 0; every other segment's parent is a lower segment of the same well.
All inputs are finite; a program needn't handle non-finite values.
Results may differ from the reference program's by a relative error of at most 0.0003.
Values sent between devices are 32-bit elements; how exact they have to be, the bound alone decides.
No kernel may reach another device: no remote copies, remote signals or barrier semaphores. Data moves between devices by JAX's collectives and lax.ppermute only.
A program may use at most 192 MiB of HBM per device.

```python
import math
import jax
import jax.numpy as jnp
from jax import lax

CZ = 8
CX = 256
CY = 256
WELLS_DEV = 192
SEG_SLAB = 2
BLOCK = 128
CAP_BLK = 2
NZ = 64
NX = 4096
NY = 256
SEG = 16
WELLS = 3072
SLOTS = 256
COLUMNS = 65536
WELL_SEGS = 384
N_AREAL = 16
N_LAYER = 8


def draw_perf_blocks(key, part):
    layers = SEG // SEG_SLAB
    owners = WELLS // WELLS_DEV
    first_key, second_key, third_key = jax.random.split(jax.random.fold_in(key, 11), 3)
    far_counts = jax.random.randint(first_key, (layers, owners, owners), 0, CAP_BLK // 2 + 1)
    near_counts = jax.random.randint(third_key, (layers, owners, owners), CAP_BLK // 2, CAP_BLK + 1)
    hot_owner = jax.random.randint(second_key, (layers,), 0, owners)
    owner_ids = jnp.arange(owners, dtype=jnp.int32)
    gap = (owner_ids[None, :] - owner_ids[:, None]) % owners
    distance = jnp.minimum(gap, owners - gap)
    counts = jnp.where(distance[None] == 0, CAP_BLK, jnp.where(distance[None] == 1, near_counts, far_counts))
    return jnp.where(owner_ids[None, None, :] == hot_owner[:, None, None], CAP_BLK, counts).astype(jnp.int32)


def draw_seg_parent(key, part):
    raw_bits = jax.random.randint(jax.random.fold_in(key, 23), (WELLS, SEG), 0, 2 ** 30)
    positions = jnp.arange(SEG, dtype=jnp.int32)[None, :]
    return jnp.where(positions > 0, raw_bits % jnp.maximum(positions, 1), 0).astype(jnp.int32)


def set_ends(entries, stream_key, low, high):
    extent = entries.shape
    index_at = [jax.random.randint(jax.random.fold_in(stream_key, axis), (), 0, extent[axis]) for axis in range(len(extent))]
    entries = entries.at[tuple(index_at)].set(low)
    longest = extent.index(max(extent))
    index_at[longest] = (index_at[longest] + 1) % extent[longest]
    return entries.at[tuple(index_at)].set(high)


def steps_of(key, extent, shards, smallest, largest):
    gain, own = 1.0, jax.random.fold_in(key, 6)
    for axis_at, parts in shards:
        heights = jnp.exp(jax.random.uniform(jax.random.fold_in(own, axis_at), (parts,), jnp.float32, smallest / len(shards), largest / len(shards)))
        gain = gain * jnp.repeat(heights, extent[axis_at] // parts).reshape([-1 if axis == axis_at else 1 for axis in range(len(extent))])
    return gain


def centred(rng, extent, scale, bound, pieces=(), kind=jnp.bfloat16):
    loudness = steps_of(rng, extent, pieces, -0.22, 0.18) if pieces else 1.0
    drawn = jax.random.normal(rng, extent, jnp.float32) * scale * loudness
    return jnp.minimum(jnp.maximum(drawn, -bound), bound).astype(kind)


def setup_inputs(seed: int = 0) -> dict:
    key_of = jax.random.split(jax.random.key(seed), 14)
    return {
        "pressure": centred(key_of[0], (NZ, NX, NY), 1.0, 6.0, ((0, 8), (1, 16)), jnp.float32),
        "saturations": jnp.clip(0.05 + 0.35 * jax.random.uniform(key_of[1], (2, NZ, NX, NY), jnp.float32) ** steps_of(key_of[1], (2, NZ, NX, NY), ((1, 8), (2, 16)), -0.2, 0.2), 0.05, 0.4),
        "old_saturations": jnp.clip(0.05 + 0.35 * jax.random.uniform(key_of[2], (2, NZ, NX, NY), jnp.float32) ** steps_of(key_of[2], (2, NZ, NX, NY), ((1, 8), (2, 16)), -0.2, 0.2), 0.05, 0.4),
        "permeability": jnp.clip(jnp.exp(math.log(5.0) - 4.6051702 * jax.random.uniform(key_of[3], (NZ, NX, NY), jnp.float32) ** steps_of(key_of[3], (NZ, NX, NY), ((0, 8), (1, 16)), -0.2, 0.2)), 0.05, 5.0),
        "pore_volume": jnp.clip(jnp.exp(math.log(2.0) - 1.3862944 * jax.random.uniform(key_of[4], (NZ, NX, NY), jnp.float32) ** steps_of(key_of[4], (NZ, NX, NY), ((0, 8), (1, 16)), -0.2, 0.2)), 0.5, 2.0),
        "perf_cell": set_ends(jax.random.randint(key_of[5], (N_LAYER, N_AREAL, N_AREAL, SLOTS), 0, COLUMNS), jax.random.fold_in(key_of[5], 1), 0, COLUMNS - 1).astype(jnp.int32),
        "perf_layer": set_ends(jax.random.randint(key_of[6], (N_LAYER, N_AREAL, N_AREAL, SLOTS), 0, CZ), jax.random.fold_in(key_of[6], 1), 0, CZ - 1).astype(jnp.int32),
        "perf_seg": set_ends(jax.random.randint(key_of[7], (N_LAYER, N_AREAL, N_AREAL, SLOTS), 0, WELL_SEGS), jax.random.fold_in(key_of[7], 1), 0, WELL_SEGS - 1).astype(jnp.int32),
        "perf_index": jnp.clip(jnp.exp(math.log(4.0) - 2.0794415 * jax.random.uniform(key_of[8], (N_LAYER, N_AREAL, N_AREAL, SLOTS), jnp.float32) ** steps_of(key_of[8], (N_LAYER, N_AREAL, N_AREAL, SLOTS), ((0, 8), (1, 16)), -0.2, 0.2)), 0.5, 4.0),
        "perf_blocks": draw_perf_blocks(jax.random.fold_in(key_of[13], 71), 0),
        "seg_parent": draw_seg_parent(jax.random.fold_in(key_of[13], 71), 0),
        "seg_cond": jnp.clip(jnp.exp(math.log(100.0) - 2.3025851 * jax.random.uniform(key_of[11], (WELLS, SEG), jnp.float32) ** steps_of(key_of[11], (WELLS, SEG), ((0, 16),), -0.2, 0.2)), 10.0, 100.0),
        "seg_target": centred(key_of[12], (WELLS, SEG), 1.0, 6.0, ((0, 16),), jnp.float32),
    }


MU_WATER = 0.5
MU_OIL = 2.0
MU_GAS = 0.2
GRAVITY = (0.35, 0.28, 0.07)
GEOMETRY = (0.4, 1.0, 1.0)
RELAX = 20.0

def mobilities(water, gas_sat):
    oil_sat = 1.0 - water - gas_sat
    return jnp.stack([water * water / MU_WATER, oil_sat * oil_sat / MU_OIL, gas_sat * gas_sat / MU_GAS])

def face(values, direction, offset, face_count):
    picks = [slice(1, -1), slice(1, -1), slice(1, -1)]
    picks[direction] = slice(offset, offset + face_count)
    leading = (slice(None),) * (values.ndim - 3)
    return values[leading + tuple(picks)]

def divergence(padded, lam_pad):
    press = padded[0]
    perm = padded[3]
    gravity = jnp.array(GRAVITY, dtype=press.dtype)[:, None, None, None]
    result = None
    for direction in range(3):
        face_count = press.shape[direction] - 1
        perm_left = face(perm, direction, 0, face_count)
        perm_right = face(perm, direction, 1, face_count)
        transmiss = GEOMETRY[direction] * 2.0 * perm_left * perm_right / (perm_left + perm_right)
        pressure_drop = face(press, direction, 0, face_count) - face(press, direction, 1, face_count)
        potential = pressure_drop[None] + (gravity if direction == 0 else 0.0 * gravity)
        mob_left = face(lam_pad, direction, 0, face_count)
        mob_right = face(lam_pad, direction, 1, face_count)
        upwind = jnp.where(potential > 0, mob_left, mob_right)
        face_flux = transmiss[None] * upwind * potential
        outflow = lax.slice_in_dim(face_flux, 1, face_count, axis=direction + 1) - lax.slice_in_dim(face_flux, 0, face_count - 1, axis=direction + 1)
        result = outflow if result is None else result + outflow
    return result

def solve_wells(seg_mobility, seg_weighted, seg_parent, seg_cond, seg_target):
    nseg = seg_parent.shape[1]
    positions = jnp.arange(nseg, dtype=jnp.int32)
    incidence = (positions[None, :, None] == positions[None, None, :]).astype(seg_cond.dtype) - (seg_parent[:, :, None] == positions[None, None, :]).astype(seg_cond.dtype)
    weight = seg_cond * (positions > 0).astype(seg_cond.dtype)[None, :]
    laplacian = jnp.einsum('bsi,bs,bsj->bij', incidence, weight, incidence, precision=lax.Precision.HIGHEST)
    matrix = laplacian + (seg_mobility + RELAX)[:, :, None] * jnp.eye(nseg, dtype=seg_cond.dtype)[None]
    right_side = seg_weighted + RELAX * seg_target
    factor = jnp.linalg.cholesky(matrix)
    return jax.scipy.linalg.cho_solve((factor, True), right_side[:, :, None])[:, :, 0]

def to_blocks(values):
    return values.reshape(N_LAYER, CZ, N_AREAL, CX, CY).transpose(0, 2, 1, 3, 4).reshape(N_LAYER, N_AREAL, CZ * CX * CY)

def from_blocks(values):
    return values.reshape(N_LAYER, N_AREAL, CZ, CX, CY).transpose(0, 2, 1, 3, 4).reshape(NZ, NX, NY)

def reference(pressure, saturations, old_saturations, permeability, pore_volume, perf_cell, perf_layer, perf_seg, perf_index, perf_blocks, seg_parent, seg_cond, seg_target):
    fields = jnp.concatenate([pressure[None], saturations, permeability[None]], axis=0)
    padded = jnp.pad(fields, ((0, 0), (1, 1), (1, 1), (1, 1)))
    lam_pad = mobilities(padded[1], padded[2])
    net_flow = divergence(padded, lam_pad)
    mobility = lam_pad[:, 1:-1, 1:-1, 1:-1]
    press_blocks = to_blocks(pressure)
    mob_blocks = jnp.stack([to_blocks(mobility[phase]) for phase in range(3)])
    slot_count = perf_cell.shape[3]
    block_cell = (perf_layer * (CX * CY) + perf_cell).astype(jnp.int32)
    flat_cells = block_cell.reshape(N_LAYER, N_AREAL, N_AREAL * slot_count)
    perf_press = jnp.take_along_axis(press_blocks, flat_cells, axis=2).reshape(perf_cell.shape)
    perf_mob = jnp.take_along_axis(mob_blocks, flat_cells[None], axis=3).reshape((3,) + perf_cell.shape)
    live_mask = (jnp.arange(slot_count, dtype=jnp.int32)[None, None, None, :] < perf_blocks[..., None] * BLOCK).astype(pressure.dtype)
    weighted = (perf_index * live_mask)[None] * perf_mob
    mobile_sum = weighted[0] + weighted[1] + weighted[2]
    owner_ids = jnp.arange(N_AREAL, dtype=jnp.int32)[None, None, :, None]
    layer_ids = jnp.arange(N_LAYER, dtype=jnp.int32)[:, None, None, None]
    source_ids = jnp.arange(N_AREAL, dtype=jnp.int32)[None, :, None, None]
    global_seg = ((owner_ids * WELLS_DEV + perf_seg // SEG_SLAB) * SEG + layer_ids * SEG_SLAB + perf_seg % SEG_SLAB).reshape(-1).astype(jnp.int32)
    seg_mobility = jax.ops.segment_sum(mobile_sum.reshape(-1), global_seg, WELLS * SEG).reshape(WELLS, SEG)
    seg_weighted = jax.ops.segment_sum((mobile_sum * perf_press).reshape(-1), global_seg, WELLS * SEG).reshape(WELLS, SEG)
    well_pressure = solve_wells(seg_mobility, seg_weighted, seg_parent, seg_cond, seg_target)
    perf_well = well_pressure.reshape(-1)[global_seg].reshape(perf_cell.shape)
    perf_rates = weighted * (perf_press - perf_well)[None]
    cell_ids = ((layer_ids * N_AREAL + source_ids) * (CZ * CX * CY) + block_cell).reshape(-1).astype(jnp.int32)
    inflow = jnp.stack([from_blocks(jax.ops.segment_sum(perf_rates[phase].reshape(-1), cell_ids, N_LAYER * N_AREAL * CZ * CX * CY)) for phase in range(3)])
    water = saturations[0]
    gas_sat = saturations[1]
    states = jnp.stack([water, 1.0 - water - gas_sat, gas_sat])
    old_states = jnp.stack([old_saturations[0], 1.0 - old_saturations[0] - old_saturations[1], old_saturations[1]])
    cell_residual = pore_volume[None] * (states - old_states) + net_flow + inflow
    return (cell_residual, well_pressure)
```

```python
import jax
import jax.numpy as jnp
from jax import lax
from jax.experimental import pallas as pl
from jax.experimental.pallas import tpu as pltpu
from jax.sharding import PartitionSpec as P

CZ = 8
CX = 256
CY = 256
LANES = 128
ROWS = CZ * CX
WELLS_DEV = 192
SEG = 16
SEG_SLAB = 2
OWNERS = 16
SLOTS = 256
ACCS = 4
N_LAYER = 8
DEVICES = OWNERS * N_LAYER
GROUP = WELLS_DEV // N_LAYER
HALF = 32

MU_WATER = 0.5
MU_OIL = 2.0
MU_GAS = 0.2
GRAVITY = (0.35, 0.28, 0.07)
GEOMETRY = (0.4, 1.0, 1.0)
RELAX = 20.0

F32 = jnp.float32
I32 = jnp.int32


def mobilities(water, gas_sat):
    oil_sat = 1.0 - water - gas_sat
    return (
        water * water * (1.0 / MU_WATER),
        oil_sat * oil_sat * (1.0 / MU_OIL),
        gas_sat * gas_sat / MU_GAS,
    )


def iota(shape, dim):
    return lax.broadcasted_iota(I32, shape, dim)


def bcast_row(ref, row):
    return jnp.broadcast_to(ref[pl.ds(row, 1), :], (8, LANES))


def split_slots(values):
    return jnp.concatenate([values[:, :LANES], values[:, LANES:]], axis=0)


def gather_kernel(
    rows_s, blocks_s, p_ref, sat_ref, lane_ref, group_ref, spot_ref, index_ref, sums_ref, pslot_ref, p_rows, m_rows
):
    layer = pl.program_id(0)
    for strip in range(0, CX, 32):
        here = pl.ds(strip, 32)
        press = p_ref[0, here, :]
        lam = mobilities(sat_ref[0, 0, here, :], sat_ref[1, 0, here, :])
        total = lam[0] + lam[1] + lam[2]
        for half in range(2):
            start = pl.multiple_of(half * ROWS + layer * CX + strip, 8)
            cols = slice(half * LANES, (half + 1) * LANES)
            p_rows[pl.ds(start, 32), :] = press[:, cols]
            m_rows[pl.ds(start, 32), :] = total[:, cols]

    @pl.when(layer == CZ - 1)
    def _():
        sub = iota((8, LANES), 0)
        lane = iota((8, LANES), 1)
        places = iota((LANES, LANES), 0)
        pslot_ref[...] = jnp.zeros_like(pslot_ref)

        def owner_step(owner, carry):
            panel = pl.ds(pl.multiple_of(owner * N_LAYER, 8), N_LAYER)
            sums_ref[panel, :] = jnp.zeros((N_LAYER, LANES), F32)
            count = blocks_s[owner]
            for half in range(2):

                @pl.when(count > half)
                def _():
                    block = half * OWNERS + owner
                    lane_of = bcast_row(lane_ref, block)
                    acc_p = jnp.zeros((8, LANES), F32)
                    acc_m = jnp.zeros((8, LANES), F32)
                    for group in range(16):
                        grp_p = None
                        grp_m = None
                        for i in range(8):
                            row = rows_s[block, 8 * group + i]
                            row_p = jnp.broadcast_to(p_rows[pl.ds(row, 1), :], (8, LANES))
                            row_m = jnp.broadcast_to(m_rows[pl.ds(row, 1), :], (8, LANES))
                            grp_p = row_p if i == 0 else jnp.where(sub == i, row_p, grp_p)
                            grp_m = row_m if i == 0 else jnp.where(sub == i, row_m, grp_m)
                        keep = lane == 8 * group + sub
                        acc_p = jnp.where(keep, jnp.take_along_axis(grp_p, lane_of, axis=1), acc_p)
                        acc_m = jnp.where(keep, jnp.take_along_axis(grp_m, lane_of, axis=1), acc_m)
                    press = jnp.sum(acc_p, axis=0, keepdims=True)
                    total = jnp.sum(acc_m, axis=0, keepdims=True)
                    pslot_ref[pl.ds(block, 1), :] = press
                    mobile = index_ref[pl.ds(block, 1), :] * total
                    group_of = bcast_row(group_ref, block) == sub
                    value = jnp.concatenate(
                        [
                            jnp.where(group_of, jnp.broadcast_to(v, (8, LANES)), 0.0)
                            for v in (mobile, mobile * press)
                        ],
                        axis=1,
                    )
                    high = value.astype(jnp.bfloat16).astype(F32)
                    rest = value - high
                    middle = rest.astype(jnp.bfloat16).astype(F32)
                    low = rest - middle
                    pieces = jnp.concatenate([high, middle, low], axis=0).astype(jnp.bfloat16)
                    spot = jnp.broadcast_to(spot_ref[pl.ds(block, 1), :], (LANES, LANES))
                    hot = jnp.concatenate([spot == places, spot == places - 2 * HALF], axis=1)
                    out = lax.dot_general(
                        pieces,
                        hot.astype(F32).astype(jnp.bfloat16),
                        (((1,), (1,)), ((), ())),
                        preferred_element_type=F32,
                    )
                    sums_ref[panel, :] += out[0:8] + out[8:16] + out[16:24]

            return carry

        lax.fori_loop(0, OWNERS, owner_step, 0)


def gather_sums(rows, blocks, pressure, saturations, lanes, groups, spots, index):
    whole = pl.BlockSpec((2 * OWNERS, LANES), lambda z, *_: (0, 0))
    return pl.pallas_call(
        gather_kernel,
        grid_spec=pltpu.PrefetchScalarGridSpec(
            num_scalar_prefetch=2,
            grid=(CZ,),
            in_specs=[
                pl.BlockSpec((1, CX, CY), lambda z, *_: (z, 0, 0)),
                pl.BlockSpec((2, 1, CX, CY), lambda z, *_: (0, z, 0, 0)),
                whole,
                whole,
                whole,
                whole,
            ],
            out_specs=[
                pl.BlockSpec((DEVICES, LANES), lambda z, *_: (0, 0)),
                whole,
            ],
            scratch_shapes=[
                pltpu.VMEM((2 * ROWS, LANES), F32),
                pltpu.VMEM((2 * ROWS, LANES), F32),
            ],
        ),
        out_shape=[
            jax.ShapeDtypeStruct((DEVICES, LANES), F32),
            jax.ShapeDtypeStruct((2 * OWNERS, LANES), F32),
        ],
        compiler_params=pltpu.CompilerParams(vmem_limit_bytes=58 << 20),
        cost_estimate=pl.CostEstimate(flops=0, bytes_accessed=24 << 20, transcendentals=0),
        name="gather_sums",
    )(rows, blocks, pressure, saturations, lanes, groups, spots, index)


def solve_kernel(sums_ref, parent_ref, cond_ref, target_ref, send_ref, parts):
    total = sums_ref[0:N_LAYER, :]
    for owner in range(1, OWNERS):
        total = total + sums_ref[owner * N_LAYER : (owner + 1) * N_LAYER, :]
    for part in range(4):
        parts[part] = pltpu.roll(total, LANES - HALF * part, 1) if part else total

    ground, load, parent, cond = [], [], [], []
    for s in range(SEG):
        z, k = divmod(s, SEG_SLAB)
        ground.append(parts[k, z : z + 1, :] + RELAX)
        load.append(parts[2 + k, z : z + 1, :] + RELAX * target_ref[s : s + 1, :])
        parent.append(parent_ref[s : s + 1, :])
        cond.append(cond_ref[s : s + 1, :])
    share, own = [None] * SEG, [None] * SEG
    for s in range(SEG - 1, 0, -1):
        inverse = 1.0 / (ground[s] + cond[s])
        share[s] = cond[s] * inverse
        own[s] = load[s] * inverse
        add_ground = share[s] * ground[s]
        add_load = share[s] * load[s]
        for j in range(s):
            hit = parent[s] == j
            ground[j] = ground[j] + jnp.where(hit, add_ground, 0.0)
            load[j] = load[j] + jnp.where(hit, add_load, 0.0)
    value = [load[0] / ground[0]]
    for s in range(1, SEG):
        above = value[0]
        for j in range(1, s):
            above = jnp.where(parent[s] == j, value[j], above)
        value.append(own[s] + share[s] * above)
    for s in range(SEG):
        z, k = divmod(s, SEG_SLAB)
        parts[k, z : z + 1, :] = value[s]
    first = iota((N_LAYER, LANES), 1) < HALF
    panel = jnp.where(first, parts[0], pltpu.roll(parts[1], HALF, 1))
    for owner in range(OWNERS):
        send_ref[owner * N_LAYER : (owner + 1) * N_LAYER, :] = panel


def solve_wells(sums, parent, cond, target):
    vmem = pl.BlockSpec(memory_space=pltpu.VMEM)
    return pl.pallas_call(
        solve_kernel,
        in_specs=[vmem] * 4,
        out_specs=vmem,
        out_shape=jax.ShapeDtypeStruct((DEVICES, LANES), F32),
        scratch_shapes=[pltpu.VMEM((4, N_LAYER, LANES), F32)],
        compiler_params=pltpu.CompilerParams(vmem_limit_bytes=4 << 20),
        cost_estimate=pl.CostEstimate(flops=0, bytes_accessed=1 << 20, transcendentals=0),
        name="solve_wells",
    )(sums, parent, cond, target)


def doubled_mobilities(water, gas_sat):
    oil_sat = 1.0 - water - gas_sat
    return (
        water * water * (2.0 / MU_WATER),
        oil_sat * oil_sat * (2.0 / MU_OIL),
        gas_sat * gas_sat * (2.0 / MU_GAS),
    )


def half_harmonic(left, right):
    return left * right / (left + right)


PLANES = CZ + 2
PAD = 8
STRIP = 32
PADDED = PAD + CX + STRIP


def flow_kernel(
    p_hbm, sat_hbm, k_hbm, below_hbm, above_hbm, west_ref, east_ref, old_ref, pore_ref, out_ref,
    cells, sats, lams, rolled, zflux, sems
):
    layer = pl.program_id(0)
    body_rows = pl.ds(PAD, CX)

    def plane_copies(sources, plane):
        targets = (
            cells.at[0, plane, body_rows, :],
            sats.at[0, plane],
            sats.at[1, plane],
            cells.at[1, plane, body_rows, :],
        )
        return [
            pltpu.make_async_copy(source, target, sems.at[plane, f])
            for f, (source, target) in enumerate(zip(sources, targets))
        ]

    def body_copies(z):
        return plane_copies((p_hbm.at[z], sat_hbm.at[0, z], sat_hbm.at[1, z], k_hbm.at[z]), z + 1)

    def halo_copies(source, plane):
        return plane_copies([source.at[f] for f in range(4)], plane)

    def vertical(low, high):
        trans = GEOMETRY[0] * half_harmonic(low[1], high[1])
        drop = low[0] - high[0]
        flux = []
        for a in range(3):
            potential = drop + GRAVITY[a]
            flux.append(trans * potential * jnp.where(potential > 0, low[2 + a], high[2 + a]))
        return flux

    def level(low, high, mask=None):
        drop = low[0] - high[0]
        rate = half_harmonic(low[1], high[1]) * drop
        if mask is not None:
            rate = jnp.where(mask, 0.0, rate)
        return [rate * jnp.where(drop > 0, low[2 + a], high[2 + a]) for a in range(3)]

    plane = layer + 1
    now = lax.rem(layer, 2)
    later = 1 - now

    def here_at(row, size):
        rows = pl.ds(row, size)
        return [cells[0, plane, rows, :], cells[1, plane, rows, :]] + [
            lams[now, a, rows, :] for a in range(3)
        ]

    @pl.when(layer == 0)
    def _():
        for copy in halo_copies(below_hbm, 0):
            copy.start()
        for z in range(CZ):
            for copy in body_copies(z):
                copy.start()
        for copy in halo_copies(above_hbm, CZ + 1):
            copy.start()
        for copy in halo_copies(below_hbm, 0) + body_copies(0):
            copy.wait()

        def first(i, carry):
            at = pl.ds(pl.multiple_of(STRIP * i, STRIP), STRIP)
            row = pl.ds(pl.multiple_of(PAD + STRIP * i, 8), STRIP)
            low = [cells[0, 0, row, :], cells[1, 0, row, :]]
            low += doubled_mobilities(sats[0, 0, at, :], sats[1, 0, at, :])
            lam = doubled_mobilities(sats[0, 1, at, :], sats[1, 1, at, :])
            flux = vertical(low, [cells[0, 1, row, :], cells[1, 1, row, :]] + list(lam))
            for a in range(3):
                lams[0, a, row, :] = lam[a]
                zflux[a, at, :] = flux[a]
            return carry

        lax.fori_loop(0, CX // STRIP, first, 0)

    @pl.when(layer < CZ - 1)
    def _():
        for copy in body_copies(layer + 1):
            copy.wait()

    @pl.when(layer == CZ - 1)
    def _():
        for copy in halo_copies(above_hbm, CZ + 1):
            copy.wait()

    for side, row in ((west_ref, PAD - 1), (east_ref, PAD + CX)):
        value = [side[f, pl.ds(layer, 1), :] for f in range(4)]
        cells[0, plane, row : row + 1, :] = value[0]
        cells[1, plane, row : row + 1, :] = value[3]
        lam = doubled_mobilities(value[1], value[2])
        for a in range(3):
            lams[now, a, row : row + 1, :] = lam[a]

    sub = iota((STRIP, CY), 0)
    top = iota((8, CY), 0) == 0
    last_lane = iota((STRIP, CY), 1) == CY - 1

    flux = level(here_at(PAD - 1, 1), here_at(PAD, 1))
    down = tuple(jnp.broadcast_to(f, (8, CY)) for f in flux)
    for f, value in enumerate(here_at(PAD, STRIP)):
        rolled[f] = pltpu.roll(value, CY - 1, 1)

    def step(i, carry):
        row = pl.multiple_of(PAD + STRIP * i, 8)
        at = pl.ds(pl.multiple_of(STRIP * i, STRIP), STRIP)
        here = here_at(row, STRIP)
        flux_y = level(here, [rolled[f] for f in range(5)], last_lane)
        back_y = [pltpu.roll(f, 1, 1) for f in flux_y]
        after = here_at(row + STRIP, STRIP)
        after_rolled = [pltpu.roll(v, CY - 1, 1) for v in after]

        neighbour = [
            jnp.where(
                sub == STRIP - 1,
                jnp.broadcast_to(n[0:1], (STRIP, CY)),
                pltpu.roll(v, STRIP - 1, 0),
            )
            for v, n in zip(here, after)
        ]
        flux_x = level(here, neighbour)
        down_x = [pltpu.roll(f, 1, 0) for f in flux_x]
        heads = tuple(d[0:8] for d in down_x)
        lam = doubled_mobilities(sats[0, plane + 1, at, :], sats[1, plane + 1, at, :])
        high = [cells[0, plane + 1, pl.ds(row, STRIP), :], cells[1, plane + 1, pl.ds(row, STRIP), :]]
        flux_z = vertical(here, high + list(lam))
        water = sats[0, plane, at, :]
        gas = sats[1, plane, at, :]
        old_water = old_ref[0, 0, at, :]
        old_gas = old_ref[1, 0, at, :]
        pore = pore_ref[0, at, :]
        change = [
            water - old_water,
            (1.0 - water - gas) - (1.0 - old_water - old_gas),
            gas - old_gas,
        ]
        for a in range(3):
            lams[later, a, pl.ds(row, STRIP), :] = lam[a]
            net = flux_z[a] - zflux[a, at, :]
            zflux[a, at, :] = flux_z[a]
            before = jnp.concatenate([jnp.where(top, carry[a], heads[a]), down_x[a][8:]], axis=0)
            net = net + (flux_x[a] - before)
            net = net + (flux_y[a] - back_y[a])
            out_ref[a, 0, at, :] = pore * change[a] + net
        for f in range(5):
            rolled[f] = after_rolled[f]
        return heads

    lax.fori_loop(0, CX // STRIP, step, down)


def cell_flows(pressure, saturations, permeability, below, above, west, east, old, pore):
    hbm = pl.BlockSpec(memory_space=pl.ANY)
    side = pl.BlockSpec((4, CZ, CY), lambda z: (0, 0, 0))
    return pl.pallas_call(
        flow_kernel,
        grid=(CZ,),
        in_specs=[hbm, hbm, hbm, hbm, hbm, side, side]
        + [
            pl.BlockSpec((2, 1, CX, CY), lambda z: (0, z, 0, 0)),
            pl.BlockSpec((1, CX, CY), lambda z: (z, 0, 0)),
        ],
        out_specs=pl.BlockSpec((3, 1, CX, CY), lambda z: (0, z, 0, 0)),
        out_shape=jax.ShapeDtypeStruct((3, CZ, CX, CY), F32),
        scratch_shapes=[
            pltpu.VMEM((2, PLANES, PADDED, CY), F32),
            pltpu.VMEM((2, PLANES, CX, CY), F32),
            pltpu.VMEM((2, 3, PADDED, CY), F32),
            pltpu.VMEM((5, STRIP, CY), F32),
            pltpu.VMEM((3, CX, CY), F32),
            pltpu.SemaphoreType.DMA((PLANES, 4)),
        ],
        compiler_params=pltpu.CompilerParams(vmem_limit_bytes=58 << 20),
        cost_estimate=pl.CostEstimate(flops=0, bytes_accessed=40 << 20, transcendentals=0),
        name="cell_flows",
    )(pressure, saturations, permeability, below, above, west, east, old, pore)


def inflow_kernel(
    rows_s, blocks_s, areal_s, pw_ref, pslot_ref, lane_ref, group_ref, spot_ref, index_ref, flow_ref, sat_ref,
    out_ref, slab_ref, rate, *sums
):
    layer = pl.program_id(0)

    @pl.when(layer == 0)
    def _():
        zero = jnp.zeros((64, LANES), F32)

        def clear(i, carry):
            for acc in sums:
                acc[pl.ds(pl.multiple_of(64 * i, 64), 64), :] = zero
            return carry

        lax.fori_loop(0, 2 * ROWS // 64, clear, 0)
        panels = [pw_ref[pl.ds(g, OWNERS, stride=N_LAYER), :] for g in range(N_LAYER)]
        for half in range(2):
            here = slice(half * OWNERS, (half + 1) * OWNERS)
            group = group_ref[here, :]
            spot = spot_ref[here, :]
            well_press = jnp.take_along_axis(panels[0], spot, axis=1)
            for g in range(1, N_LAYER):
                well_press = jnp.where(
                    group == g, jnp.take_along_axis(panels[g], spot, axis=1), well_press
                )
            rate[here, :] = index_ref[here, :] * (pslot_ref[here, :] - well_press)

        sub = iota((8, LANES), 0)
        lane = iota((8, LANES), 1)

        mine = pw_ref[pl.ds(pl.multiple_of(areal_s[0] * N_LAYER, 8), N_LAYER), :]
        for tile in range(2):
            well = lane + tile * LANES
            group = lax.shift_right_logical(well * 2731, 16)
            for k in range(SEG_SLAB):
                spot = jnp.minimum(well - group * GROUP + k * HALF, LANES - 1)
                value = jnp.where(group == sub, jnp.take_along_axis(mine, spot, axis=1), 0.0)
                value = jnp.sum(value, axis=0, keepdims=True)
                width = min(LANES, WELLS_DEV - tile * LANES)
                slab_ref[k : k + 1, tile * LANES : tile * LANES + width] = value[:, :width]

        def owner_step(owner, carry):
            count = blocks_s[owner]
            for half in range(2):

                @pl.when(count > half)
                def _():
                    block = half * OWNERS + owner
                    lane_of = bcast_row(lane_ref, block)
                    rate_of = bcast_row(rate, block)
                    for group in range(16):
                        pick = sub + 8 * group
                        place = jnp.take_along_axis(lane_of, pick, axis=1)
                        value = jnp.take_along_axis(rate_of, pick, axis=1)
                        value = jnp.where(lane == place, value, 0.0)
                        for i in range(8):
                            row = rows_s[block, 8 * group + i]
                            acc = sums[i % ACCS]
                            acc[pl.ds(row, 1), :] += value[i : i + 1, :]

            return carry

        lax.fori_loop(0, OWNERS, owner_step, 0)

    for strip in range(0, CX, 16):
        here = pl.ds(strip, 16)
        lam = mobilities(sat_ref[0, 0, here, :], sat_ref[1, 0, here, :])
        halves = []
        for half in range(2):
            start = pl.multiple_of(half * ROWS + layer * CX + strip, 8)
            total = sums[0][pl.ds(start, 16), :]
            for acc in sums[1:]:
                total = total + acc[pl.ds(start, 16), :]
            halves.append(total)
        total = jnp.concatenate(halves, axis=1)
        for a in range(3):
            out_ref[a, 0, here, :] = flow_ref[a, 0, here, :] + lam[a] * total


def add_inflow(rows, blocks, areal, pw, pslot, lanes, groups, spots, index, flow, saturations):
    whole = pl.BlockSpec((2 * OWNERS, LANES), lambda z, *_: (0, 0))
    flow_spec = pl.BlockSpec((3, 1, CX, CY), lambda z, *_: (0, z, 0, 0))
    return pl.pallas_call(
        inflow_kernel,
        grid_spec=pltpu.PrefetchScalarGridSpec(
            num_scalar_prefetch=3,
            grid=(CZ,),
            in_specs=[
                pl.BlockSpec((DEVICES, LANES), lambda z, *_: (0, 0)),
                whole,
                whole,
                whole,
                whole,
                whole,
                flow_spec,
                pl.BlockSpec((2, 1, CX, CY), lambda z, *_: (0, z, 0, 0)),
            ],
            out_specs=[flow_spec, pl.BlockSpec((SEG_SLAB, WELLS_DEV), lambda z, *_: (0, 0))],
            scratch_shapes=[pltpu.VMEM((2 * OWNERS, LANES), F32)]
            + [pltpu.VMEM((2 * ROWS, LANES), F32) for _ in range(ACCS)],
        ),
        out_shape=[
            jax.ShapeDtypeStruct((3, CZ, CX, CY), F32),
            jax.ShapeDtypeStruct((SEG_SLAB, WELLS_DEV), F32),
        ],
        compiler_params=pltpu.CompilerParams(vmem_limit_bytes=58 << 20),
        cost_estimate=pl.CostEstimate(flops=0, bytes_accessed=24 << 20, transcendentals=0),
        name="add_inflow",
    )(rows, blocks, areal, pw, pslot, lanes, groups, spots, index, flow, saturations)


def on_device(
    pressure,
    saturations,
    old_saturations,
    permeability,
    pore_volume,
    perf_cell,
    perf_layer,
    perf_seg,
    perf_index,
    perf_blocks,
    seg_parent,
    seg_cond,
    seg_target,
):
    n_areal = lax.axis_size("areal")
    n_layer = lax.axis_size("layer")
    up_a = [(i, i + 1) for i in range(n_areal - 1)]
    up_l = [(i, i + 1) for i in range(n_layer - 1)]
    down_a = [(j, i) for i, j in up_a]
    down_l = [(j, i) for i, j in up_l]
    fields = (pressure, saturations[0], saturations[1], permeability)

    cell = split_slots(perf_cell[0, 0])
    lanes = cell & (LANES - 1)
    rows = ((cell >> 7) & 1) * ROWS + split_slots(perf_layer[0, 0]) * CX + (cell >> 8)
    blocks = perf_blocks[0, 0]
    seg = split_slots(perf_seg[0, 0])
    well = seg >> 1
    groups = (well * 2731) >> 16
    spots = well - groups * GROUP + (seg & 1) * HALF
    index = split_slots(perf_index[0, 0])

    sums, pslot = gather_sums(rows, blocks, pressure, saturations, lanes, groups, spots, index)
    received = lax.all_to_all(sums, ("areal", "layer"), split_axis=0, concat_axis=0, tiled=True)

    layer = lax.axis_index("layer").astype(I32)
    areal = lax.axis_index("areal").astype(I32).reshape(1)

    def own_wells(values):
        part = lax.dynamic_slice_in_dim(values, layer * GROUP, GROUP, axis=0)
        return jnp.pad(part.T, ((0, 0), (0, LANES - GROUP)))

    systems = [own_wells(v) for v in (seg_parent, seg_cond, seg_target)]
    west = lax.ppermute(jnp.stack([f[:, CX - 1, :] for f in fields]), "areal", up_a)
    east = lax.ppermute(jnp.stack([f[:, 0, :] for f in fields]), "areal", down_a)
    below = lax.ppermute(jnp.stack([f[CZ - 1] for f in fields]), "layer", up_l)
    above = lax.ppermute(jnp.stack([f[0] for f in fields]), "layer", down_l)
    flow = cell_flows(
        pressure, saturations, permeability, below, above, west, east, old_saturations, pore_volume
    )

    send = solve_wells(received, *systems)
    pw = lax.all_to_all(send, ("areal", "layer"), split_axis=0, concat_axis=0, tiled=True)
    residual, slab = add_inflow(
        rows, blocks, areal, pw, pslot, lanes, groups, spots, index, flow, saturations
    )
    return residual, slab.T


def solution(mesh):
    return jax.shard_map(
        on_device,
        mesh=mesh,
        in_specs=(
            P("layer", "areal", None),
            P(None, "layer", "areal", None),
            P(None, "layer", "areal", None),
            P("layer", "areal", None),
            P("layer", "areal", None),
            P("layer", "areal", None, None),
            P("layer", "areal", None, None),
            P("layer", "areal", None, None),
            P("layer", "areal", None, None),
            P("layer", "areal", None),
            P("areal", None),
            P("areal", None),
            P("areal", None),
        ),
        out_specs=(P(None, "layer", "areal", None), P("areal", "layer")),
        check_vma=False,
    )
```

```python
import functools

import jax
import jax.numpy as jnp
from jax import lax
from jax.experimental import pallas as pl
from jax.experimental.pallas import tpu as pltpu
from jax.sharding import PartitionSpec as P


CZ = 8
CX = 256
CY = 256
LANES = 128
ROWS = CZ * CX
WELLS_DEV = 192
SEG = 16
SEG_SLAB = 2
OWNERS = 16
ACCS = 4
N_LAYER = 8
DEVICES = OWNERS * N_LAYER
GROUP = WELLS_DEV // N_LAYER
HALF = 32
UNROLL = 4
VMEM_KERNEL = 26 << 20

MU_WATER = 0.5
MU_OIL = 2.0
MU_GAS = 0.2
GRAVITY = (0.35, 0.28, 0.07)
GEOMETRY = (0.4, 1.0, 1.0)
RELAX = 20.0

F32 = jnp.float32
I32 = jnp.int32


def mobilities(water, gas_sat):
    oil_sat = 1.0 - water - gas_sat
    return (
        water * water * (1.0 / MU_WATER),
        oil_sat * oil_sat * (1.0 / MU_OIL),
        gas_sat * gas_sat / MU_GAS,
    )


def in_hbm(value):
    return pltpu.with_memory_space_constraint(value, pltpu.HBM)


def iota(shape, dim):
    return lax.broadcasted_iota(I32, shape, dim)


def bcast_row(ref, row):
    return jnp.broadcast_to(ref[pl.ds(row, 1), :], (8, LANES))


def gather_kernel(
    blocks_s, p_hbm, sat_hbm, cell_ref, depth_ref, seg_ref, index_ref,
    sums_ref, rows_ref, ints_ref, floats_ref, p_rows, sat_rows, m_rows, p_groups, m_groups, rows_s, sem, sems
):
    to_smem = pltpu.make_async_copy(rows_ref, rows_s, sem)
    copies = []
    for z in range(CZ):
        for half in range(2):
            cols = pl.ds(half * LANES, LANES)
            at = pl.ds(half * ROWS + z * CX, CX)
            copies.append(
                [
                    pltpu.make_async_copy(
                        sat_hbm.at[0, z, :, cols], sat_rows.at[0, at, :], sems.at[z, half, 0]
                    ),
                    pltpu.make_async_copy(
                        sat_hbm.at[1, z, :, cols], sat_rows.at[1, at, :], sems.at[z, half, 1]
                    ),
                    pltpu.make_async_copy(
                        p_hbm.at[z, :, cols], p_rows.at[at, :], sems.at[z, half, 2]
                    ),
                ]
            )
            for copy in copies[-1]:
                copy.start()

    for half in range(2):
        cols = slice(half * LANES, (half + 1) * LANES)
        here = slice(half * OWNERS, (half + 1) * OWNERS)
        cell = cell_ref[0, 0, :, cols]
        seg = seg_ref[0, 0, :, cols]
        well = lax.shift_right_logical(seg, 1)
        group = lax.shift_right_logical(well * 2731, 16)
        rows_ref[here, :] = (
            (lax.shift_right_logical(cell, 7) & 1) * ROWS
            + depth_ref[0, 0, :, cols] * CX
            + lax.shift_right_logical(cell, 8)
        )
        ints_ref[0, here, :] = cell & (LANES - 1)
        ints_ref[1, here, :] = group
        ints_ref[2, here, :] = well - group * GROUP + (seg & 1) * HALF
        floats_ref[0, here, :] = index_ref[0, 0, :, cols]
    to_smem.start()

    for z in range(CZ):
        for half in range(2):
            for copy in copies[2 * z + half]:
                copy.wait()

            def dense(i, carry):
                at = pl.ds(pl.multiple_of(half * ROWS + z * CX + 64 * i, 64), 64)
                lam = mobilities(sat_rows[0, at, :], sat_rows[1, at, :])
                m_rows[at, :] = lam[0] + lam[1] + lam[2]
                return carry

            lax.fori_loop(0, CX // 64, dense, 0)

    to_smem.wait()
    sub = iota((8, LANES), 0)
    lane = iota((8, LANES), 1)
    places = iota((LANES, LANES), 0)

    def pick(owner, carry):
        for half in range(2):

            @pl.when(blocks_s[owner] > half)
            def _():
                block = half * OWNERS + owner
                for group in range(16):
                    grp_p = None
                    grp_m = None
                    for i in range(8):
                        row = rows_s[block, 8 * group + i]
                        row_p = jnp.broadcast_to(p_rows[pl.ds(row, 1), :], (8, LANES))
                        row_m = jnp.broadcast_to(m_rows[pl.ds(row, 1), :], (8, LANES))
                        grp_p = row_p if i == 0 else jnp.where(sub == i, row_p, grp_p)
                        grp_m = row_m if i == 0 else jnp.where(sub == i, row_m, grp_m)
                    p_groups[block, 8 * group : 8 * group + 8, :] = grp_p
                    m_groups[block, 8 * group : 8 * group + 8, :] = grp_m

        return carry

    lax.fori_loop(0, OWNERS, pick, 0)

    def reduce(step, carry):
        for unit in range(UNROLL):
            owner = step * UNROLL + unit
            count = blocks_s[owner]
            values = []
            hots = []
            for half in range(2):
                block = half * OWNERS + owner
                lane_of = jnp.broadcast_to(ints_ref[0, pl.ds(block, 1), :], (8, LANES))
                acc_p = jnp.zeros((8, LANES), F32)
                acc_m = jnp.zeros((8, LANES), F32)
                for group in range(16):
                    keep = lane == 8 * group + sub
                    at = slice(8 * group, 8 * group + 8)
                    grp_p = jnp.take_along_axis(p_groups[block, at, :], lane_of, axis=1)
                    grp_m = jnp.take_along_axis(m_groups[block, at, :], lane_of, axis=1)
                    acc_p = jnp.where(keep, grp_p, acc_p)
                    acc_m = jnp.where(keep, grp_m, acc_m)
                live = count > half
                press = jnp.where(live, jnp.sum(acc_p, axis=0, keepdims=True), 0.0)
                total = jnp.where(live, jnp.sum(acc_m, axis=0, keepdims=True), 0.0)
                floats_ref[1, pl.ds(block, 1), :] = press
                mobile = floats_ref[0, pl.ds(block, 1), :] * total
                group_of = jnp.broadcast_to(ints_ref[1, pl.ds(block, 1), :], (8, LANES)) == sub
                for v in (mobile, mobile * press):
                    values.append(jnp.where(group_of, jnp.broadcast_to(v, (8, LANES)), 0.0))
                spot = jnp.broadcast_to(ints_ref[2, pl.ds(block, 1), :], (LANES, LANES))
                hots += [spot == places, spot == places - 2 * HALF]
            value = jnp.concatenate(values, axis=1)
            high = value.astype(jnp.bfloat16).astype(F32)
            rest = value - high
            middle = rest.astype(jnp.bfloat16).astype(F32)
            low = rest - middle
            pieces = jnp.concatenate([high, middle, low], axis=0).astype(jnp.bfloat16)
            hot = jnp.concatenate(hots, axis=1).astype(F32).astype(jnp.bfloat16)
            out = lax.dot_general(
                pieces, hot, (((1,), (1,)), ((), ())), preferred_element_type=F32
            )
            panel = pl.ds(pl.multiple_of(owner * N_LAYER, 8), N_LAYER)
            sums_ref[panel, :] = out[0:8] + out[8:16] + out[16:24]
        return carry

    lax.fori_loop(0, OWNERS // UNROLL, reduce, 0)


def gather_sums(blocks, pressure, saturations, cell, depth, seg, index):
    hbm = pl.BlockSpec(memory_space=pl.ANY)
    vmem = pl.BlockSpec(memory_space=pltpu.VMEM)
    return pl.pallas_call(
        gather_kernel,
        in_specs=[pl.BlockSpec(memory_space=pltpu.SMEM), hbm, hbm] + [vmem] * 4,
        out_specs=[vmem] * 4,
        out_shape=[
            jax.ShapeDtypeStruct((DEVICES, LANES), F32),
            jax.ShapeDtypeStruct((2 * OWNERS, LANES), I32),
            jax.ShapeDtypeStruct((3, 2 * OWNERS, LANES), I32),
            jax.ShapeDtypeStruct((2, 2 * OWNERS, LANES), F32),
        ],
        scratch_shapes=[
            pltpu.VMEM((2 * ROWS, LANES), F32),
            pltpu.VMEM((2, 2 * ROWS, LANES), F32),
            pltpu.VMEM((2 * ROWS, LANES), F32),
            pltpu.VMEM((2 * OWNERS, LANES, LANES), F32),
            pltpu.VMEM((2 * OWNERS, LANES, LANES), F32),
            pltpu.SMEM((2 * OWNERS, LANES), I32),
            pltpu.SemaphoreType.DMA(()),
            pltpu.SemaphoreType.DMA((CZ, 2, 3)),
        ],
        compiler_params=pltpu.CompilerParams(vmem_limit_bytes=VMEM_KERNEL),
        cost_estimate=pl.CostEstimate(flops=0, bytes_accessed=24 << 20, transcendentals=0),
        name="gather_sums",
    )(blocks, in_hbm(pressure), in_hbm(saturations), cell, depth, seg, index)


def pack_kernel(
    parity_s, p_hbm, sat_hbm, k_hbm, plane_even_ref, plane_odd_ref, row_even_ref, row_odd_ref, edges, sems
):
    z_odd, x_odd = parity_s[0], parity_s[1]
    sources = (p_hbm, sat_hbm.at[0], sat_hbm.at[1], k_hbm)
    planes, sides = [], []
    for f, source in enumerate(sources):
        first = (1 - z_odd) * (CZ - 1)
        planes.append(
            pltpu.make_async_copy(source.at[first], plane_even_ref.at[f], sems.at[0, f])
        )
        planes.append(
            pltpu.make_async_copy(source.at[CZ - 1 - first], plane_odd_ref.at[f], sems.at[1, f])
        )
        for side, row in ((0, CX - 8), (1, 0)):
            sides.append(
                pltpu.make_async_copy(
                    source.at[:, pl.ds(row, 8), :], edges.at[side, f], sems.at[2 + side, f]
                )
            )
    for copy in sides + planes:
        copy.start()
    for copy in sides:
        copy.wait()
    swap = x_odd == 1
    for f in range(4):
        for z in range(CZ):
            last = edges[0, f, z, 7:8, :]
            first = edges[1, f, z, 0:1, :]
            row_even_ref[f, z : z + 1, :] = jnp.where(swap, first, last)
            row_odd_ref[f, z : z + 1, :] = jnp.where(swap, last, first)
    for copy in planes:
        copy.wait()


def pack_halos(parity, pressure, saturations, permeability):
    hbm = pl.BlockSpec(memory_space=pl.ANY)
    vmem = pl.BlockSpec(memory_space=pltpu.VMEM)
    return pl.pallas_call(
        pack_kernel,
        in_specs=[pl.BlockSpec(memory_space=pltpu.SMEM)] + [hbm] * 3,
        out_specs=[vmem] * 4,
        out_shape=[
            jax.ShapeDtypeStruct((4, CX, CY), F32),
            jax.ShapeDtypeStruct((4, CX, CY), F32),
            jax.ShapeDtypeStruct((4, CZ, CY), F32),
            jax.ShapeDtypeStruct((4, CZ, CY), F32),
        ],
        scratch_shapes=[
            pltpu.VMEM((2, 4, CZ, 8, CY), F32),
            pltpu.SemaphoreType.DMA((4, 4)),
        ],
        compiler_params=pltpu.CompilerParams(vmem_limit_bytes=VMEM_KERNEL),
        cost_estimate=pl.CostEstimate(flops=0, bytes_accessed=6 << 20, transcendentals=0),
        name="pack_halos",
    )(parity, in_hbm(pressure), in_hbm(saturations), in_hbm(permeability))


def solve_kernel(sums_ref, parent_ref, cond_ref, target_ref, send_ref, parts):
    total = sums_ref[0:N_LAYER, :]
    for owner in range(1, OWNERS):
        total = total + sums_ref[owner * N_LAYER : (owner + 1) * N_LAYER, :]
    for part in range(4):
        parts[part] = pltpu.roll(total, LANES - HALF * part, 1) if part else total

    ground, load, parent, cond = [], [], [], []
    for s in range(SEG):
        z, k = divmod(s, SEG_SLAB)
        ground.append(parts[k, z : z + 1, :] + RELAX)
        load.append(parts[2 + k, z : z + 1, :] + RELAX * target_ref[s : s + 1, :])
        parent.append(parent_ref[s : s + 1, :])
        cond.append(cond_ref[s : s + 1, :])
    share, own = [None] * SEG, [None] * SEG
    for s in range(SEG - 1, 0, -1):
        inverse = 1.0 / (ground[s] + cond[s])
        share[s] = cond[s] * inverse
        own[s] = load[s] * inverse
        add_ground = share[s] * ground[s]
        add_load = share[s] * load[s]
        for j in range(s):
            hit = parent[s] == j
            ground[j] = ground[j] + jnp.where(hit, add_ground, 0.0)
            load[j] = load[j] + jnp.where(hit, add_load, 0.0)
    value = [load[0] / ground[0]]
    for s in range(1, SEG):
        above = value[0]
        for j in range(1, s):
            above = jnp.where(parent[s] == j, value[j], above)
        value.append(own[s] + share[s] * above)
    for s in range(SEG):
        z, k = divmod(s, SEG_SLAB)
        parts[k, z : z + 1, :] = value[s]
    first = iota((N_LAYER, LANES), 1) < HALF
    panel = jnp.where(first, parts[0], pltpu.roll(parts[1], HALF, 1))
    for owner in range(OWNERS):
        send_ref[owner * N_LAYER : (owner + 1) * N_LAYER, :] = panel


def solve_wells(sums, parent, cond, target):
    vmem = pl.BlockSpec(memory_space=pltpu.VMEM)
    return pl.pallas_call(
        solve_kernel,
        in_specs=[vmem] * 4,
        out_specs=vmem,
        out_shape=jax.ShapeDtypeStruct((DEVICES, LANES), F32),
        scratch_shapes=[pltpu.VMEM((4, N_LAYER, LANES), F32)],
        compiler_params=pltpu.CompilerParams(vmem_limit_bytes=4 << 20),
        cost_estimate=pl.CostEstimate(flops=0, bytes_accessed=1 << 20, transcendentals=0),
        name="solve_wells",
    )(sums, parent, cond, target)


def doubled_mobilities(water, gas_sat):
    oil_sat = 1.0 - water - gas_sat
    return (
        water * water * (2.0 / MU_WATER),
        oil_sat * oil_sat * (2.0 / MU_OIL),
        gas_sat * gas_sat * (2.0 / MU_GAS),
    )


def half_harmonic(left, right):
    return left * right / (left + right)


STRIP = 32


def wide(ref, *index):
    *lead, start, size = index
    return jnp.concatenate(
        [ref[(*lead, pl.ds(half * ROWS + start, size), slice(None))] for half in range(2)], axis=1
    )


def flow_kernel(
    z0, nz, parity_s, p_hbm, sat_hbm, k_hbm, plane_even_ref, plane_odd_ref, row_even_ref, row_odd_ref,
    old_ref, pore_ref, out_ref,
    cells, lams, rolled, zflux, sems
):
    step_at = pl.program_id(0)
    layer = step_at + z0
    now = lax.rem(step_at, 2)
    later = 1 - now
    halo_below = z0 == 0
    first_plane = z0 if halo_below else z0 - 1
    last_plane = z0 + nz if halo_below else z0 + nz - 1

    def plane_copies(z):
        sources = (p_hbm.at[z], sat_hbm.at[0, z], sat_hbm.at[1, z], k_hbm.at[z])
        return [
            pltpu.make_async_copy(source, cells.at[f, z], sems.at[z, f])
            for f, source in enumerate(sources)
        ]

    def vertical(low, high):
        trans = GEOMETRY[0] * half_harmonic(low[1], high[1])
        drop = low[0] - high[0]
        flux = []
        for a in range(3):
            potential = drop + GRAVITY[a]
            flux.append(trans * potential * jnp.where(potential > 0, low[2 + a], high[2 + a]))
        return flux

    def level(low, high, mask=None):
        drop = low[0] - high[0]
        rate = half_harmonic(low[1], high[1]) * drop
        if mask is not None:
            rate = jnp.where(mask, 0.0, rate)
        return [rate * jnp.where(drop > 0, low[2 + a], high[2 + a]) for a in range(3)]

    def cell_at(z, row, size):
        rows = pl.ds(row, size)
        return (
            [cells[0, z, rows, :], cells[3, z, rows, :]],
            [cells[1, z, rows, :], cells[2, z, rows, :]],
        )

    halo_from_even = parity_s[0] == (1 if halo_below else 0)

    def halo_at(row, size):
        rows = pl.ds(row, size)
        value = [
            jnp.where(halo_from_even, plane_even_ref[f, rows, :], plane_odd_ref[f, rows, :])
            for f in range(4)
        ]
        return [value[0], value[3]], [value[1], value[2]]

    def here_at(row, size):
        rows = pl.ds(row, size)
        return [cells[0, layer, rows, :], cells[3, layer, rows, :]] + [
            lams[now, a, rows, :] for a in range(3)
        ]

    @pl.when(step_at == 0)
    def _():
        for z in range(first_plane, last_plane + 1):
            for copy in plane_copies(z):
                copy.start()
        for z in range(first_plane, z0 + 1):
            for copy in plane_copies(z):
                copy.wait()

        def first(i, carry):
            row = pl.multiple_of(STRIP * i, STRIP)
            low, low_sat = halo_at(row, STRIP) if halo_below else cell_at(z0 - 1, row, STRIP)
            high, high_sat = cell_at(z0, row, STRIP)
            lam = doubled_mobilities(*high_sat)
            flux = vertical(low + list(doubled_mobilities(*low_sat)), high + list(lam))
            for a in range(3):
                lams[0, a, pl.ds(row, STRIP), :] = lam[a]
                zflux[a, pl.ds(row, STRIP), :] = flux[a]
            return carry

        lax.fori_loop(0, CX // STRIP, first, 0)

    sub = iota((STRIP, CY), 0)
    top = iota((8, CY), 0) == 0
    last_lane = iota((STRIP, CY), 1) == CY - 1

    def side_row(from_even):
        here = pl.ds(layer, 1)
        value = [
            jnp.where(from_even, row_even_ref[f, here, :], row_odd_ref[f, here, :])
            for f in range(4)
        ]
        return [value[0], value[3]] + list(doubled_mobilities(value[1], value[2]))

    east = side_row(parity_s[1] == 0)
    flux = level(side_row(parity_s[1] == 1), [v[0:1] for v in here_at(0, 8)])
    down = tuple(jnp.broadcast_to(f, (8, CY)) for f in flux)
    for f, value in enumerate(here_at(0, STRIP)):
        rolled[f] = pltpu.roll(value, CY - 1, 1)

    def sweep(next_at):
        def step(i, carry):
            row = pl.multiple_of(STRIP * i, STRIP)
            at = pl.ds(row, STRIP)
            final = i == CX // STRIP - 1
            here = here_at(row, STRIP)
            flux_y = level(here, [rolled[f] for f in range(5)], last_lane)
            back_y = [pltpu.roll(f, 1, 1) for f in flux_y]
            after = here_at(
                pl.multiple_of(jnp.minimum(row + STRIP, CX - STRIP), STRIP), STRIP
            )
            after_rolled = [pltpu.roll(v, CY - 1, 1) for v in after]
            neighbour = [
                jnp.where(
                    sub == STRIP - 1,
                    jnp.broadcast_to(jnp.where(final, e, n[0:1]), (STRIP, CY)),
                    pltpu.roll(v, STRIP - 1, 0),
                )
                for v, n, e in zip(here, after, east)
            ]
            flux_x = level(here, neighbour)
            down_x = [pltpu.roll(f, 1, 0) for f in flux_x]
            heads = tuple(d[0:8] for d in down_x)
            high, high_sat = next_at(row, STRIP)
            lam = doubled_mobilities(*high_sat)
            flux_z = vertical(here, high + list(lam))
            water = cells[1, layer, at, :]
            gas = cells[2, layer, at, :]
            old_water = old_ref[0, 0, at, :]
            old_gas = old_ref[1, 0, at, :]
            pore = pore_ref[0, at, :]
            change = [
                water - old_water,
                (1.0 - water - gas) - (1.0 - old_water - old_gas),
                gas - old_gas,
            ]
            for a in range(3):
                lams[later, a, at, :] = lam[a]
                net = flux_z[a] - zflux[a, at, :]
                zflux[a, at, :] = flux_z[a]
                before = jnp.concatenate(
                    [jnp.where(top, carry[a], heads[a]), down_x[a][8:]], axis=0
                )
                net = net + (flux_x[a] - before)
                net = net + (flux_y[a] - back_y[a])
                out_ref[a, 0, at, :] = pore * change[a] + net
            for f in range(5):
                rolled[f] = after_rolled[f]
            return heads

        lax.fori_loop(0, CX // STRIP, step, down)

    inside = nz if halo_below else nz - 1

    @pl.when(step_at < inside)
    def _():
        for copy in plane_copies(layer + 1):
            copy.wait()
        sweep(lambda row, size: cell_at(layer + 1, row, size))

    if not halo_below:

        @pl.when(step_at == inside)
        def _():
            sweep(halo_at)


def cell_flows(z0, nz, parity, pressure, saturations, permeability, planes, sides, old, pore):
    hbm = pl.BlockSpec(memory_space=pl.ANY)
    vmem = pl.BlockSpec(memory_space=pltpu.VMEM)
    return pl.pallas_call(
        functools.partial(flow_kernel, z0, nz),
        grid=(nz,),
        in_specs=[pl.BlockSpec(memory_space=pltpu.SMEM), hbm, hbm, hbm, vmem, vmem, vmem, vmem]
        + [
            pl.BlockSpec((2, 1, CX, CY), lambda z: (0, z + z0, 0, 0)),
            pl.BlockSpec((1, CX, CY), lambda z: (z + z0, 0, 0)),
        ],
        out_specs=pl.BlockSpec((3, 1, CX, CY), lambda z: (0, z, 0, 0)),
        out_shape=pltpu.HBM((3, nz, CX, CY), F32),
        scratch_shapes=[
            pltpu.VMEM((4, CZ, CX, CY), F32),
            pltpu.VMEM((2, 3, CX, CY), F32),
            pltpu.VMEM((5, STRIP, CY), F32),
            pltpu.VMEM((3, CX, CY), F32),
            pltpu.SemaphoreType.DMA((CZ, 4)),
        ],
        compiler_params=pltpu.CompilerParams(vmem_limit_bytes=VMEM_KERNEL),
        cost_estimate=pl.CostEstimate(flops=0, bytes_accessed=20 << 20, transcendentals=0),
    )(
        parity, in_hbm(pressure), in_hbm(saturations), in_hbm(permeability), *planes, *sides, in_hbm(old), in_hbm(pore)
    )


def inflow_kernel(
    rows_s, blocks_s, areal_s, pw_ref, ints_ref, floats_ref, low_hbm, high_hbm, sat_hbm,
    out_ref, slab_ref, rate, flows, sats, sems, *sums
):
    layer = pl.program_id(0)

    def layer_copies(source, at, z):
        return [
            pltpu.make_async_copy(source.at[a, at], flows.at[a, z], sems.at[z, a]) for a in range(3)
        ] + [
            pltpu.make_async_copy(sat_hbm.at[a, z], sats.at[a, z], sems.at[z, 3 + a]) for a in range(2)
        ]

    @pl.when(layer == 0)
    def _():
        for z in range(CZ):
            source = low_hbm if z < CZ // 2 else high_hbm
            for copy in layer_copies(source, z % (CZ // 2), z):
                copy.start()
        zero = jnp.zeros((64, LANES), F32)

        def clear(i, carry):
            for acc in sums:
                acc[pl.ds(pl.multiple_of(64 * i, 64), 64), :] = zero
            return carry

        lax.fori_loop(0, 2 * ROWS // 64, clear, 0)
        panels = [pw_ref[pl.ds(g, OWNERS, stride=N_LAYER), :] for g in range(N_LAYER)]
        for half in range(2):
            here = slice(half * OWNERS, (half + 1) * OWNERS)
            group = ints_ref[1, here, :]
            spot = ints_ref[2, here, :]
            well_press = jnp.take_along_axis(panels[0], spot, axis=1)
            for g in range(1, N_LAYER):
                well_press = jnp.where(
                    group == g, jnp.take_along_axis(panels[g], spot, axis=1), well_press
                )
            rate[here, :] = floats_ref[0, here, :] * (floats_ref[1, here, :] - well_press)

        sub = iota((8, LANES), 0)
        lane = iota((8, LANES), 1)

        mine = pw_ref[pl.ds(pl.multiple_of(areal_s[0] * N_LAYER, 8), N_LAYER), :]
        for tile in range(2):
            well = lane + tile * LANES
            group = lax.shift_right_logical(well * 2731, 16)
            for k in range(SEG_SLAB):
                spot = jnp.minimum(well - group * GROUP + k * HALF, LANES - 1)
                value = jnp.where(group == sub, jnp.take_along_axis(mine, spot, axis=1), 0.0)
                value = jnp.sum(value, axis=0, keepdims=True)
                width = min(LANES, WELLS_DEV - tile * LANES)
                slab_ref[k : k + 1, tile * LANES : tile * LANES + width] = value[:, :width]

        def owner_step(owner, carry):
            count = blocks_s[owner]
            for half in range(2):

                @pl.when(count > half)
                def _():
                    block = half * OWNERS + owner
                    lane_of = jnp.broadcast_to(ints_ref[0, pl.ds(block, 1), :], (8, LANES))
                    rate_of = bcast_row(rate, block)
                    for group in range(16):
                        pick = sub + 8 * group
                        place = jnp.take_along_axis(lane_of, pick, axis=1)
                        value = jnp.take_along_axis(rate_of, pick, axis=1)
                        value = jnp.where(lane == place, value, 0.0)
                        for i in range(8):
                            row = rows_s[block, 8 * group + i]
                            acc = sums[i % ACCS]
                            acc[pl.ds(row, 1), :] += value[i : i + 1, :]

            return carry

        lax.fori_loop(0, OWNERS, owner_step, 0)

    for copy in layer_copies(low_hbm, 0, layer):
        copy.wait()

    def combine(i, carry):
        row = pl.multiple_of(32 * i, 32)
        here = pl.ds(row, 32)
        base = pl.multiple_of(layer * CX + row, 8)
        lam = mobilities(sats[0, layer, here, :], sats[1, layer, here, :])
        total = wide(sums[0], base, 32)
        for acc in sums[1:]:
            total = total + wide(acc, base, 32)
        for a in range(3):
            out_ref[a, 0, here, :] = flows[a, layer, here, :] + lam[a] * total
        return carry

    lax.fori_loop(0, CX // 32, combine, 0)


def add_inflow(rows, blocks, areal, pw, ints, floats, low, high, saturations):
    hbm = pl.BlockSpec(memory_space=pl.ANY)
    flow_spec = pl.BlockSpec((3, 1, CX, CY), lambda z, *_: (0, z, 0, 0))
    return pl.pallas_call(
        inflow_kernel,
        grid_spec=pltpu.PrefetchScalarGridSpec(
            num_scalar_prefetch=3,
            grid=(CZ,),
            in_specs=[
                pl.BlockSpec((DEVICES, LANES), lambda z, *_: (0, 0)),
                pl.BlockSpec((3, 2 * OWNERS, LANES), lambda z, *_: (0, 0, 0)),
                pl.BlockSpec((2, 2 * OWNERS, LANES), lambda z, *_: (0, 0, 0)),
                hbm,
                hbm,
                hbm,
            ],
            out_specs=[flow_spec, pl.BlockSpec((SEG_SLAB, WELLS_DEV), lambda z, *_: (0, 0))],
            scratch_shapes=[
                pltpu.VMEM((2 * OWNERS, LANES), F32),
                pltpu.VMEM((3, CZ, CX, CY), F32),
                pltpu.VMEM((2, CZ, CX, CY), F32),
                pltpu.SemaphoreType.DMA((CZ, 5)),
            ]
            + [pltpu.VMEM((2 * ROWS, LANES), F32) for _ in range(ACCS)],
        ),
        out_shape=[
            jax.ShapeDtypeStruct((3, CZ, CX, CY), F32),
            jax.ShapeDtypeStruct((SEG_SLAB, WELLS_DEV), F32),
        ],
        compiler_params=pltpu.CompilerParams(vmem_limit_bytes=VMEM_KERNEL),
        cost_estimate=pl.CostEstimate(flops=0, bytes_accessed=24 << 20, transcendentals=0),
        name="add_inflow",
    )(rows, blocks, areal, pw, ints, floats, in_hbm(low), in_hbm(high), in_hbm(saturations))


def on_device(
    pressure,
    saturations,
    old_saturations,
    permeability,
    pore_volume,
    perf_cell,
    perf_layer,
    perf_seg,
    perf_index,
    perf_blocks,
    seg_parent,
    seg_cond,
    seg_target,
):
    n_areal = lax.axis_size("areal")
    n_layer = lax.axis_size("layer")
    layer = lax.axis_index("layer").astype(I32)
    areal = lax.axis_index("areal").astype(I32).reshape(1)
    blocks = perf_blocks[0, 0]
    depth = CZ // 2
    parity = jnp.concatenate([layer.reshape(1), areal]) & 1

    def own_wells(values):
        part = lax.dynamic_slice_in_dim(values, layer * GROUP, GROUP, axis=0)
        return jnp.pad(part.T, ((0, 0), (0, LANES - GROUP)))

    def flows(z0):
        return cell_flows(
            z0, depth, parity, pressure, saturations, permeability, planes, sides, old_saturations, pore_volume
        )

    def even_swap(values, axis, count):
        return lax.ppermute(values, axis, [(i, i ^ 1) for i in range(count)])

    def odd_swap(values, axis, count):
        pairs = [(i, i + 1) for i in range(1, count - 1, 2)]
        return lax.ppermute(values, axis, pairs + [(j, i) for i, j in pairs])

    def exchange(values):
        return lax.all_to_all(values, ("areal", "layer"), split_axis=0, concat_axis=0, tiled=True)

    packed = pack_halos(parity, pressure, saturations, permeability)
    plane_even = even_swap(packed[0], "layer", n_layer)
    plane_odd = odd_swap(packed[1], "layer", n_layer)
    row_even = even_swap(packed[2], "areal", n_areal)
    row_odd = odd_swap(packed[3], "areal", n_areal)
    planes, sides = (plane_even, plane_odd), (row_even, row_odd)
    sums, rows, ints, floats = gather_sums(
        blocks, pressure, saturations, perf_cell, perf_layer, perf_seg, perf_index
    )
    received = exchange(sums)
    low = flows(0)
    systems = [own_wells(v) for v in (seg_parent, seg_cond, seg_target)]
    solved = solve_wells(received, *systems)
    pw = exchange(solved)
    high = flows(depth)
    residual, slab = add_inflow(rows, blocks, areal, pw, ints, floats, low, high, saturations)
    return residual, slab.T


def solution(mesh):
    return jax.shard_map(
        on_device,
        mesh=mesh,
        in_specs=(
            P("layer", "areal", None),
            P(None, "layer", "areal", None),
            P(None, "layer", "areal", None),
            P("layer", "areal", None),
            P("layer", "areal", None),
            P("layer", "areal", None, None),
            P("layer", "areal", None, None),
            P("layer", "areal", None, None),
            P("layer", "areal", None, None),
            P("layer", "areal", None),
            P("areal", None),
            P("areal", None),
            P("areal", None),
        ),
        out_specs=(P(None, "layer", "areal", None), P("areal", "layer")),
        check_vma=False,
    )
```

```python
import jax
import jax.numpy as jnp
from jax import lax
from jax.experimental import pallas as pl
from jax.experimental.pallas import tpu as pltpu
from jax.sharding import PartitionSpec as P


CZ = 8
CX = 256
CY = 256
LANES = 128
ROWS = CZ * CX
WELLS_DEV = 192
SEG = 16
SEG_SLAB = 2
OWNERS = 16
ACCS = 4
N_LAYER = 8
DEVICES = OWNERS * N_LAYER
GROUP = WELLS_DEV // N_LAYER
HALF = 32
UNROLL = 4

MU_WATER = 0.5
MU_OIL = 2.0
MU_GAS = 0.2
GRAVITY = (0.35, 0.28, 0.07)
GEOMETRY = (0.4, 1.0, 1.0)
RELAX = 20.0

F32 = jnp.float32
I32 = jnp.int32


def mobilities(water, gas_sat):
    oil_sat = 1.0 - water - gas_sat
    return (
        water * water * (1.0 / MU_WATER),
        oil_sat * oil_sat * (1.0 / MU_OIL),
        gas_sat * gas_sat / MU_GAS,
    )


def in_hbm(value):
    return pltpu.with_memory_space_constraint(value, pltpu.HBM)


def in_vmem(value):
    return pltpu.with_memory_space_constraint(value, pltpu.VMEM)


def iota(shape, dim):
    return lax.broadcasted_iota(I32, shape, dim)


def bcast_row(ref, row):
    return jnp.broadcast_to(ref[pl.ds(row, 1), :], (8, LANES))


def gather_kernel(
    blocks_s, p_ref, sat_ref, cell_ref, depth_ref, seg_ref, index_ref,
    sums_ref, rows_ref, ints_ref, floats_ref, p_rows, m_rows, p_groups, m_groups, rows_s, sem
):
    to_smem = pltpu.make_async_copy(rows_ref, rows_s, sem)
    for half in range(2):
        cols = slice(half * LANES, (half + 1) * LANES)
        here = slice(half * OWNERS, (half + 1) * OWNERS)
        cell = cell_ref[0, 0, :, cols]
        seg = seg_ref[0, 0, :, cols]
        well = lax.shift_right_logical(seg, 1)
        group = lax.shift_right_logical(well * 2731, 16)
        rows_ref[here, :] = (
            (lax.shift_right_logical(cell, 7) & 1) * ROWS
            + depth_ref[0, 0, :, cols] * CX
            + lax.shift_right_logical(cell, 8)
        )
        ints_ref[0, here, :] = cell & (LANES - 1)
        ints_ref[1, here, :] = group
        ints_ref[2, here, :] = well - group * GROUP + (seg & 1) * HALF
        floats_ref[0, here, :] = index_ref[0, 0, :, cols]
    to_smem.start()

    def dense(i, carry):
        z = lax.div(i, CX // 32)
        row = pl.multiple_of((i - z * (CX // 32)) * 32, 32)
        here = pl.ds(row, 32)
        press = p_ref[z, here, :]
        lam = mobilities(sat_ref[0, z, here, :], sat_ref[1, z, here, :])
        total = lam[0] + lam[1] + lam[2]
        for half in range(2):
            at = pl.ds(pl.multiple_of(half * ROWS + 32 * i, 32), 32)
            cols = slice(half * LANES, (half + 1) * LANES)
            p_rows[at, :] = press[:, cols]
            m_rows[at, :] = total[:, cols]
        return carry

    lax.fori_loop(0, CZ * CX // 32, dense, 0)
    to_smem.wait()
    sub = iota((8, LANES), 0)
    lane = iota((8, LANES), 1)
    places = iota((LANES, LANES), 0)

    def pick(owner, carry):
        for half in range(2):

            @pl.when(blocks_s[owner] > half)
            def _():
                block = half * OWNERS + owner
                for group in range(16):
                    grp_p = None
                    grp_m = None
                    for i in range(8):
                        row = rows_s[block, 8 * group + i]
                        row_p = jnp.broadcast_to(p_rows[pl.ds(row, 1), :], (8, LANES))
                        row_m = jnp.broadcast_to(m_rows[pl.ds(row, 1), :], (8, LANES))
                        grp_p = row_p if i == 0 else jnp.where(sub == i, row_p, grp_p)
                        grp_m = row_m if i == 0 else jnp.where(sub == i, row_m, grp_m)
                    p_groups[block, 8 * group : 8 * group + 8, :] = grp_p
                    m_groups[block, 8 * group : 8 * group + 8, :] = grp_m

        return carry

    lax.fori_loop(0, OWNERS, pick, 0)

    def reduce(step, carry):
        for unit in range(UNROLL):
            owner = step * UNROLL + unit
            count = blocks_s[owner]
            values = []
            hots = []
            for half in range(2):
                block = half * OWNERS + owner
                lane_of = jnp.broadcast_to(ints_ref[0, pl.ds(block, 1), :], (8, LANES))
                acc_p = jnp.zeros((8, LANES), F32)
                acc_m = jnp.zeros((8, LANES), F32)
                for group in range(16):
                    keep = lane == 8 * group + sub
                    at = slice(8 * group, 8 * group + 8)
                    grp_p = jnp.take_along_axis(p_groups[block, at, :], lane_of, axis=1)
                    grp_m = jnp.take_along_axis(m_groups[block, at, :], lane_of, axis=1)
                    acc_p = jnp.where(keep, grp_p, acc_p)
                    acc_m = jnp.where(keep, grp_m, acc_m)
                live = count > half
                press = jnp.where(live, jnp.sum(acc_p, axis=0, keepdims=True), 0.0)
                total = jnp.where(live, jnp.sum(acc_m, axis=0, keepdims=True), 0.0)
                floats_ref[1, pl.ds(block, 1), :] = press
                mobile = floats_ref[0, pl.ds(block, 1), :] * total
                group_of = jnp.broadcast_to(ints_ref[1, pl.ds(block, 1), :], (8, LANES)) == sub
                for v in (mobile, mobile * press):
                    values.append(jnp.where(group_of, jnp.broadcast_to(v, (8, LANES)), 0.0))
                spot = jnp.broadcast_to(ints_ref[2, pl.ds(block, 1), :], (LANES, LANES))
                hots += [spot == places, spot == places - 2 * HALF]
            value = jnp.concatenate(values, axis=1)
            high = value.astype(jnp.bfloat16).astype(F32)
            rest = value - high
            middle = rest.astype(jnp.bfloat16).astype(F32)
            low = rest - middle
            pieces = jnp.concatenate([high, middle, low], axis=0).astype(jnp.bfloat16)
            hot = jnp.concatenate(hots, axis=1).astype(F32).astype(jnp.bfloat16)
            out = lax.dot_general(
                pieces, hot, (((1,), (1,)), ((), ())), preferred_element_type=F32
            )
            panel = pl.ds(pl.multiple_of(owner * N_LAYER, 8), N_LAYER)
            sums_ref[panel, :] = out[0:8] + out[8:16] + out[16:24]
        return carry

    lax.fori_loop(0, OWNERS // UNROLL, reduce, 0)


def gather_sums(blocks, pressure, saturations, cell, depth, seg, index):
    vmem = pl.BlockSpec(memory_space=pltpu.VMEM)
    return pl.pallas_call(
        gather_kernel,
        in_specs=[pl.BlockSpec(memory_space=pltpu.SMEM)] + [vmem] * 6,
        out_specs=[vmem] * 4,
        out_shape=[
            jax.ShapeDtypeStruct((DEVICES, LANES), F32),
            jax.ShapeDtypeStruct((2 * OWNERS, LANES), I32),
            jax.ShapeDtypeStruct((3, 2 * OWNERS, LANES), I32),
            jax.ShapeDtypeStruct((2, 2 * OWNERS, LANES), F32),
        ],
        scratch_shapes=[
            pltpu.VMEM((2 * ROWS, LANES), F32),
            pltpu.VMEM((2 * ROWS, LANES), F32),
            pltpu.VMEM((2 * OWNERS, LANES, LANES), F32),
            pltpu.VMEM((2 * OWNERS, LANES, LANES), F32),
            pltpu.SMEM((2 * OWNERS, LANES), I32),
            pltpu.SemaphoreType.DMA(()),
        ],
        compiler_params=pltpu.CompilerParams(vmem_limit_bytes=10 << 20),
        cost_estimate=pl.CostEstimate(flops=0, bytes_accessed=24 << 20, transcendentals=0),
        name="gather_sums",
    )(blocks, in_vmem(pressure), in_vmem(saturations), cell, depth, seg, index)


def pack_kernel(
    parity_s, p_hbm, sat_hbm, k_hbm, plane_even_ref, plane_odd_ref, row_even_ref, row_odd_ref, edges, sems
):
    z_odd, x_odd = parity_s[0], parity_s[1]
    sources = (p_hbm, sat_hbm.at[0], sat_hbm.at[1], k_hbm)
    planes, sides = [], []
    for f, source in enumerate(sources):
        first = (1 - z_odd) * (CZ - 1)
        planes.append(
            pltpu.make_async_copy(source.at[first], plane_even_ref.at[f], sems.at[0, f])
        )
        planes.append(
            pltpu.make_async_copy(source.at[CZ - 1 - first], plane_odd_ref.at[f], sems.at[1, f])
        )
        for side, row in ((0, CX - 8), (1, 0)):
            sides.append(
                pltpu.make_async_copy(
                    source.at[:, pl.ds(row, 8), :], edges.at[side, f], sems.at[2 + side, f]
                )
            )
    for copy in sides + planes:
        copy.start()
    for copy in sides:
        copy.wait()
    swap = x_odd == 1
    for f in range(4):
        for z in range(CZ):
            last = edges[0, f, z, 7:8, :]
            first = edges[1, f, z, 0:1, :]
            row_even_ref[f, z : z + 1, :] = jnp.where(swap, first, last)
            row_odd_ref[f, z : z + 1, :] = jnp.where(swap, last, first)
    for copy in planes:
        copy.wait()


def pack_halos(parity, pressure, saturations, permeability):
    hbm = pl.BlockSpec(memory_space=pl.ANY)
    vmem = pl.BlockSpec(memory_space=pltpu.VMEM)
    return pl.pallas_call(
        pack_kernel,
        in_specs=[pl.BlockSpec(memory_space=pltpu.SMEM)] + [hbm] * 3,
        out_specs=[vmem] * 4,
        out_shape=[
            pltpu.VMEM((4, CX, CY), F32),
            pltpu.VMEM((4, CX, CY), F32),
            jax.ShapeDtypeStruct((4, CZ, CY), F32),
            jax.ShapeDtypeStruct((4, CZ, CY), F32),
        ],
        scratch_shapes=[
            pltpu.VMEM((2, 4, CZ, 8, CY), F32),
            pltpu.SemaphoreType.DMA((4, 4)),
        ],
        compiler_params=pltpu.CompilerParams(vmem_limit_bytes=4 << 20),
        cost_estimate=pl.CostEstimate(flops=0, bytes_accessed=6 << 20, transcendentals=0),
        name="pack_halos",
    )(parity, in_hbm(pressure), in_hbm(saturations), in_hbm(permeability))


def solve_kernel(sums_ref, parent_ref, cond_ref, target_ref, send_ref, parts):
    total = sums_ref[0:N_LAYER, :]
    for owner in range(1, OWNERS):
        total = total + sums_ref[owner * N_LAYER : (owner + 1) * N_LAYER, :]
    for part in range(4):
        parts[part] = pltpu.roll(total, LANES - HALF * part, 1) if part else total

    ground, load, parent, cond = [], [], [], []
    for s in range(SEG):
        z, k = divmod(s, SEG_SLAB)
        ground.append(parts[k, z : z + 1, :] + RELAX)
        load.append(parts[2 + k, z : z + 1, :] + RELAX * target_ref[s : s + 1, :])
        parent.append(parent_ref[s : s + 1, :])
        cond.append(cond_ref[s : s + 1, :])
    share, own = [None] * SEG, [None] * SEG
    for s in range(SEG - 1, 0, -1):
        inverse = 1.0 / (ground[s] + cond[s])
        share[s] = cond[s] * inverse
        own[s] = load[s] * inverse
        add_ground = share[s] * ground[s]
        add_load = share[s] * load[s]
        for j in range(s):
            hit = parent[s] == j
            ground[j] = ground[j] + jnp.where(hit, add_ground, 0.0)
            load[j] = load[j] + jnp.where(hit, add_load, 0.0)
    value = [load[0] / ground[0]]
    for s in range(1, SEG):
        above = value[0]
        for j in range(1, s):
            above = jnp.where(parent[s] == j, value[j], above)
        value.append(own[s] + share[s] * above)
    for s in range(SEG):
        z, k = divmod(s, SEG_SLAB)
        parts[k, z : z + 1, :] = value[s]
    first = iota((N_LAYER, LANES), 1) < HALF
    panel = jnp.where(first, parts[0], pltpu.roll(parts[1], HALF, 1))
    for owner in range(OWNERS):
        send_ref[owner * N_LAYER : (owner + 1) * N_LAYER, :] = panel


def solve_wells(sums, parent, cond, target):
    vmem = pl.BlockSpec(memory_space=pltpu.VMEM)
    return pl.pallas_call(
        solve_kernel,
        in_specs=[vmem] * 4,
        out_specs=vmem,
        out_shape=jax.ShapeDtypeStruct((DEVICES, LANES), F32),
        scratch_shapes=[pltpu.VMEM((4, N_LAYER, LANES), F32)],
        compiler_params=pltpu.CompilerParams(vmem_limit_bytes=4 << 20),
        cost_estimate=pl.CostEstimate(flops=0, bytes_accessed=1 << 20, transcendentals=0),
        name="solve_wells",
    )(sums, parent, cond, target)


def doubled_mobilities(water, gas_sat):
    oil_sat = 1.0 - water - gas_sat
    return (
        water * water * (2.0 / MU_WATER),
        oil_sat * oil_sat * (2.0 / MU_OIL),
        gas_sat * gas_sat * (2.0 / MU_GAS),
    )


def half_harmonic(left, right):
    return left * right / (left + right)


STRIP = 32


def wide(ref, *index):
    *lead, start, size = index
    return jnp.concatenate(
        [ref[(*lead, pl.ds(half * ROWS + start, size), slice(None))] for half in range(2)], axis=1
    )


def flow_kernel(
    parity_s, p_hbm, sat_hbm, k_hbm, plane_even_ref, plane_odd_ref, row_even_ref, row_odd_ref,
    old_ref, pore_ref, out_ref,
    cells, lams, rolled, zflux, sems
):
    layer = pl.program_id(0)
    now = lax.rem(layer, 2)
    later = 1 - now

    def plane_copies(z):
        sources = (p_hbm.at[z], sat_hbm.at[0, z], sat_hbm.at[1, z], k_hbm.at[z])
        return [
            pltpu.make_async_copy(source, cells.at[f, z], sems.at[z, f])
            for f, source in enumerate(sources)
        ]

    def vertical(low, high):
        trans = GEOMETRY[0] * half_harmonic(low[1], high[1])
        drop = low[0] - high[0]
        flux = []
        for a in range(3):
            potential = drop + GRAVITY[a]
            flux.append(trans * potential * jnp.where(potential > 0, low[2 + a], high[2 + a]))
        return flux

    def level(low, high, mask=None):
        drop = low[0] - high[0]
        rate = half_harmonic(low[1], high[1]) * drop
        if mask is not None:
            rate = jnp.where(mask, 0.0, rate)
        return [rate * jnp.where(drop > 0, low[2 + a], high[2 + a]) for a in range(3)]

    def cell_at(z, row, size):
        rows = pl.ds(row, size)
        return (
            [cells[0, z, rows, :], cells[3, z, rows, :]],
            [cells[1, z, rows, :], cells[2, z, rows, :]],
        )

    def halo_at(from_even, row, size):
        rows = pl.ds(row, size)
        value = [
            jnp.where(from_even, plane_even_ref[f, rows, :], plane_odd_ref[f, rows, :])
            for f in range(4)
        ]
        return [value[0], value[3]], [value[1], value[2]]

    def here_at(row, size):
        rows = pl.ds(row, size)
        return [cells[0, layer, rows, :], cells[3, layer, rows, :]] + [
            lams[now, a, rows, :] for a in range(3)
        ]

    @pl.when(layer == 0)
    def _():
        for z in range(CZ):
            for copy in plane_copies(z):
                copy.start()
        for copy in plane_copies(0):
            copy.wait()

        def first(i, carry):
            row = pl.multiple_of(STRIP * i, STRIP)
            low, low_sat = halo_at(parity_s[0] == 1, row, STRIP)
            high, high_sat = cell_at(0, row, STRIP)
            lam = doubled_mobilities(*high_sat)
            flux = vertical(low + list(doubled_mobilities(*low_sat)), high + list(lam))
            for a in range(3):
                lams[0, a, pl.ds(row, STRIP), :] = lam[a]
                zflux[a, pl.ds(row, STRIP), :] = flux[a]
            return carry

        lax.fori_loop(0, CX // STRIP, first, 0)

    top = iota((8, CY), 0) == 0
    last_lane = iota((STRIP, CY), 1) == CY - 1

    def side_row(from_even):
        here = pl.ds(layer, 1)
        value = [
            jnp.where(from_even, row_even_ref[f, here, :], row_odd_ref[f, here, :])
            for f in range(4)
        ]
        return [value[0], value[3]] + list(doubled_mobilities(value[1], value[2]))

    east = [jnp.broadcast_to(v, (8, CY)) for v in side_row(parity_s[1] == 0)]
    flux = level(side_row(parity_s[1] == 1), [v[0:1] for v in here_at(0, 8)])
    down = tuple(jnp.broadcast_to(f, (8, CY)) for f in flux)
    for f, value in enumerate(here_at(0, STRIP)):
        rolled[f] = pltpu.roll(value, CY - 1, 1)

    def sweep(next_at):
        def step(i, carry):
            row = pl.multiple_of(STRIP * i, STRIP)
            at = pl.ds(row, STRIP)
            final = i == CX // STRIP - 1
            here = here_at(row, STRIP)
            flux_y = level(here, [rolled[f] for f in range(5)], last_lane)
            back_y = [pltpu.roll(f, 1, 1) for f in flux_y]
            after = here_at(
                pl.multiple_of(jnp.minimum(row + STRIP, CX - STRIP), STRIP), STRIP
            )
            after_rolled = [pltpu.roll(v, CY - 1, 1) for v in after]
            neighbour = []
            for v, n, e in zip(here, after, east):
                edge = jnp.where(final, e, n[0:8])
                longer = jnp.concatenate([v, edge], axis=0)
                neighbour.append(pltpu.roll(longer, STRIP + 7, 0)[0:STRIP])
            flux_x = level(here, neighbour)
            down_x = [pltpu.roll(f, 1, 0) for f in flux_x]
            heads = tuple(d[0:8] for d in down_x)
            high, high_sat = next_at(row, STRIP)
            lam = doubled_mobilities(*high_sat)
            flux_z = vertical(here, high + list(lam))
            water = cells[1, layer, at, :]
            gas = cells[2, layer, at, :]
            old_water = old_ref[0, 0, at, :]
            old_gas = old_ref[1, 0, at, :]
            pore = pore_ref[0, at, :]
            change = [
                water - old_water,
                (1.0 - water - gas) - (1.0 - old_water - old_gas),
                gas - old_gas,
            ]
            for a in range(3):
                lams[later, a, at, :] = lam[a]
                net = flux_z[a] - zflux[a, at, :]
                zflux[a, at, :] = flux_z[a]
                before = jnp.concatenate(
                    [jnp.where(top, carry[a], heads[a]), down_x[a][8:]], axis=0
                )
                net = net + (flux_x[a] - before)
                net = net + (flux_y[a] - back_y[a])
                out_ref[a, 0, at, :] = pore * change[a] + net
            for f in range(5):
                rolled[f] = after_rolled[f]
            return heads

        lax.fori_loop(0, CX // STRIP, step, down)

    @pl.when(layer < CZ - 1)
    def _():
        for copy in plane_copies(layer + 1):
            copy.wait()
        sweep(lambda row, size: cell_at(layer + 1, row, size))

    @pl.when(layer == CZ - 1)
    def _():
        sweep(lambda row, size: halo_at(parity_s[0] == 0, row, size))


def cell_flows(parity, pressure, saturations, permeability, planes, sides, old, pore):
    hbm = pl.BlockSpec(memory_space=pl.ANY)
    vmem = pl.BlockSpec(memory_space=pltpu.VMEM)
    return pl.pallas_call(
        flow_kernel,
        grid=(CZ,),
        in_specs=[pl.BlockSpec(memory_space=pltpu.SMEM), hbm, hbm, hbm, vmem, vmem, vmem, vmem]
        + [
            pl.BlockSpec((2, 1, CX, CY), lambda z: (0, z, 0, 0)),
            pl.BlockSpec((1, CX, CY), lambda z: (z, 0, 0)),
        ],
        out_specs=pl.BlockSpec((3, 1, CX, CY), lambda z: (0, z, 0, 0)),
        out_shape=pltpu.HBM((3, CZ, CX, CY), F32),
        scratch_shapes=[
            pltpu.VMEM((4, CZ, CX, CY), F32),
            pltpu.VMEM((2, 3, CX, CY), F32),
            pltpu.VMEM((5, STRIP, CY), F32),
            pltpu.VMEM((3, CX, CY), F32),
            pltpu.SemaphoreType.DMA((CZ, 4)),
        ],
        compiler_params=pltpu.CompilerParams(vmem_limit_bytes=16 << 20),
        cost_estimate=pl.CostEstimate(flops=0, bytes_accessed=20 << 20, transcendentals=0),
        name="cell_flows",
    )(
        parity, in_hbm(pressure), in_hbm(saturations), in_hbm(permeability), *planes, *sides, in_hbm(old), in_hbm(pore)
    )


def inflow_kernel(
    rows_s, blocks_s, areal_s, pw_ref, ints_ref, floats_ref, flow_hbm, sat_hbm,
    out_ref, slab_ref, rate, flows, sats, sems, *sums
):
    layer = pl.program_id(0)

    def layer_copies(z):
        return [
            pltpu.make_async_copy(flow_hbm.at[a, z], flows.at[a, z], sems.at[z, a]) for a in range(3)
        ] + [
            pltpu.make_async_copy(sat_hbm.at[a, z], sats.at[a, z], sems.at[z, 3 + a]) for a in range(2)
        ]

    @pl.when(layer == 0)
    def _():
        for z in range(CZ):
            for copy in layer_copies(z):
                copy.start()
        zero = jnp.zeros((64, LANES), F32)

        def clear(i, carry):
            for acc in sums:
                acc[pl.ds(pl.multiple_of(64 * i, 64), 64), :] = zero
            return carry

        lax.fori_loop(0, 2 * ROWS // 64, clear, 0)
        panels = [pw_ref[pl.ds(g, OWNERS, stride=N_LAYER), :] for g in range(N_LAYER)]
        for half in range(2):
            here = slice(half * OWNERS, (half + 1) * OWNERS)
            group = ints_ref[1, here, :]
            spot = ints_ref[2, here, :]
            well_press = jnp.take_along_axis(panels[0], spot, axis=1)
            for g in range(1, N_LAYER):
                well_press = jnp.where(
                    group == g, jnp.take_along_axis(panels[g], spot, axis=1), well_press
                )
            rate[here, :] = floats_ref[0, here, :] * (floats_ref[1, here, :] - well_press)

        sub = iota((8, LANES), 0)
        lane = iota((8, LANES), 1)

        mine = pw_ref[pl.ds(pl.multiple_of(areal_s[0] * N_LAYER, 8), N_LAYER), :]
        for tile in range(2):
            well = lane + tile * LANES
            group = lax.shift_right_logical(well * 2731, 16)
            for k in range(SEG_SLAB):
                spot = jnp.minimum(well - group * GROUP + k * HALF, LANES - 1)
                value = jnp.where(group == sub, jnp.take_along_axis(mine, spot, axis=1), 0.0)
                value = jnp.sum(value, axis=0, keepdims=True)
                width = min(LANES, WELLS_DEV - tile * LANES)
                slab_ref[k : k + 1, tile * LANES : tile * LANES + width] = value[:, :width]

        def owner_step(owner, carry):
            count = blocks_s[owner]
            for half in range(2):

                @pl.when(count > half)
                def _():
                    block = half * OWNERS + owner
                    lane_of = jnp.broadcast_to(ints_ref[0, pl.ds(block, 1), :], (8, LANES))
                    rate_of = bcast_row(rate, block)
                    for group in range(16):
                        pick = sub + 8 * group
                        place = jnp.take_along_axis(lane_of, pick, axis=1)
                        value = jnp.take_along_axis(rate_of, pick, axis=1)
                        value = jnp.where(lane == place, value, 0.0)
                        for i in range(8):
                            row = rows_s[block, 8 * group + i]
                            acc = sums[i % ACCS]
                            acc[pl.ds(row, 1), :] += value[i : i + 1, :]

            return carry

        lax.fori_loop(0, OWNERS, owner_step, 0)

    for copy in layer_copies(layer):
        copy.wait()

    def combine(i, carry):
        row = pl.multiple_of(32 * i, 32)
        here = pl.ds(row, 32)
        base = pl.multiple_of(layer * CX + row, 8)
        lam = mobilities(sats[0, layer, here, :], sats[1, layer, here, :])
        total = wide(sums[0], base, 32)
        for acc in sums[1:]:
            total = total + wide(acc, base, 32)
        for a in range(3):
            out_ref[a, 0, here, :] = flows[a, layer, here, :] + lam[a] * total
        return carry

    lax.fori_loop(0, CX // 32, combine, 0)


def add_inflow(rows, blocks, areal, pw, ints, floats, flow, saturations):
    hbm = pl.BlockSpec(memory_space=pl.ANY)
    flow_spec = pl.BlockSpec((3, 1, CX, CY), lambda z, *_: (0, z, 0, 0))
    return pl.pallas_call(
        inflow_kernel,
        grid_spec=pltpu.PrefetchScalarGridSpec(
            num_scalar_prefetch=3,
            grid=(CZ,),
            in_specs=[
                pl.BlockSpec((DEVICES, LANES), lambda z, *_: (0, 0)),
                pl.BlockSpec((3, 2 * OWNERS, LANES), lambda z, *_: (0, 0, 0)),
                pl.BlockSpec((2, 2 * OWNERS, LANES), lambda z, *_: (0, 0, 0)),
                hbm,
                hbm,
            ],
            out_specs=[flow_spec, pl.BlockSpec((SEG_SLAB, WELLS_DEV), lambda z, *_: (0, 0))],
            scratch_shapes=[
                pltpu.VMEM((2 * OWNERS, LANES), F32),
                pltpu.VMEM((3, CZ, CX, CY), F32),
                pltpu.VMEM((2, CZ, CX, CY), F32),
                pltpu.SemaphoreType.DMA((CZ, 5)),
            ]
            + [pltpu.VMEM((2 * ROWS, LANES), F32) for _ in range(ACCS)],
        ),
        out_shape=[
            jax.ShapeDtypeStruct((3, CZ, CX, CY), F32),
            jax.ShapeDtypeStruct((SEG_SLAB, WELLS_DEV), F32),
        ],
        compiler_params=pltpu.CompilerParams(vmem_limit_bytes=24 << 20),
        cost_estimate=pl.CostEstimate(flops=0, bytes_accessed=24 << 20, transcendentals=0),
        name="add_inflow",
    )(rows, blocks, areal, pw, ints, floats, in_hbm(flow), in_hbm(saturations))


def on_device(
    pressure,
    saturations,
    old_saturations,
    permeability,
    pore_volume,
    perf_cell,
    perf_layer,
    perf_seg,
    perf_index,
    perf_blocks,
    seg_parent,
    seg_cond,
    seg_target,
):
    n_areal = lax.axis_size("areal")
    n_layer = lax.axis_size("layer")
    layer = lax.axis_index("layer").astype(I32)
    areal = lax.axis_index("areal").astype(I32).reshape(1)
    blocks = perf_blocks[0, 0]
    parity = jnp.concatenate([layer.reshape(1), areal]) & 1

    def own_wells(values):
        part = lax.dynamic_slice_in_dim(values, layer * GROUP, GROUP, axis=0)
        return jnp.pad(part.T, ((0, 0), (0, LANES - GROUP)))

    def even_swap(values, axis, count):
        return lax.ppermute(values, axis, [(i, i ^ 1) for i in range(count)])

    def odd_swap(values, axis, count):
        pairs = [(i, i + 1) for i in range(1, count - 1, 2)]
        return lax.ppermute(values, axis, pairs + [(j, i) for i, j in pairs])

    def exchange(values):
        return lax.all_to_all(values, ("areal", "layer"), split_axis=0, concat_axis=0, tiled=True)

    packed = pack_halos(parity, pressure, saturations, permeability)
    sums, rows, ints, floats = gather_sums(
        blocks, pressure, saturations, perf_cell, perf_layer, perf_seg, perf_index
    )
    received = exchange(sums)
    plane_even = even_swap(packed[0], "layer", n_layer)
    plane_odd = odd_swap(packed[1], "layer", n_layer)
    row_even = even_swap(packed[2], "areal", n_areal)
    row_odd = odd_swap(packed[3], "areal", n_areal)
    planes, sides = (plane_even, plane_odd), (row_even, row_odd)
    systems = [own_wells(v) for v in (seg_parent, seg_cond, seg_target)]
    solved = solve_wells(received, *systems)
    pw = exchange(solved)
    flow = cell_flows(
        parity, pressure, saturations, permeability, planes, sides, old_saturations, pore_volume
    )
    residual, slab = add_inflow(
        rows, blocks, areal, pw, ints, floats, flow, saturations
    )
    return residual, slab.T


def solution(mesh):
    return jax.shard_map(
        on_device,
        mesh=mesh,
        in_specs=(
            P("layer", "areal", None),
            P(None, "layer", "areal", None),
            P(None, "layer", "areal", None),
            P("layer", "areal", None),
            P("layer", "areal", None),
            P("layer", "areal", None, None),
            P("layer", "areal", None, None),
            P("layer", "areal", None, None),
            P("layer", "areal", None, None),
            P("layer", "areal", None),
            P("areal", None),
            P("areal", None),
            P("areal", None),
        ),
        out_specs=(P(None, "layer", "areal", None), P("areal", "layer")),
        check_vma=False,
    )
```

```python
import jax
import jax.numpy as jnp
from jax import lax
from jax.experimental import pallas as pl
from jax.experimental.pallas import tpu as pltpu
from jax.sharding import PartitionSpec as P


CZ = 8
CX = 256
CY = 256
LANES = 128
ROWS = CZ * CX
WELLS_DEV = 192
SEG = 16
SEG_SLAB = 2
OWNERS = 16
SLOTS = 256
ACCS = 4
N_LAYER = 8
DEVICES = OWNERS * N_LAYER
GROUP = WELLS_DEV // N_LAYER
HALF = 32
UNROLL = 4

MU_WATER = 0.5
MU_OIL = 2.0
MU_GAS = 0.2
GRAVITY = (0.35, 0.28, 0.07)
GEOMETRY = (0.4, 1.0, 1.0)
RELAX = 20.0

F32 = jnp.float32
I32 = jnp.int32


def mobilities(water, gas_sat):
    oil_sat = 1.0 - water - gas_sat
    return (
        water * water * (1.0 / MU_WATER),
        oil_sat * oil_sat * (1.0 / MU_OIL),
        gas_sat * gas_sat / MU_GAS,
    )


def in_hbm(value):
    return pltpu.with_memory_space_constraint(value, pltpu.HBM)


def iota(shape, dim):
    return lax.broadcasted_iota(I32, shape, dim)


def bcast_row(ref, row):
    return jnp.broadcast_to(ref[pl.ds(row, 1), :], (8, LANES))


def gather_kernel(
    blocks_s, parity_s, p_hbm, sat_hbm, k_hbm, cell_hbm, depth_hbm, seg_hbm, index_hbm,
    sums_ref, rows_ref, ints_ref, floats_ref, plane_even_hbm, plane_odd_hbm, row_even_ref, row_odd_ref,
    p_cells, sat_cells, p_rows, m_rows, p_groups, m_groups, rows_s, edges, planes, slots, index_slots,
    sem, sems, edge_sems, plane_sems, slot_sems
):
    to_smem = pltpu.make_async_copy(rows_ref, rows_s, sem)
    slots_in = [
        pltpu.make_async_copy(source.at[0, 0], slots.at[f], slot_sems.at[f])
        for f, source in enumerate((cell_hbm, depth_hbm, seg_hbm))
    ] + [pltpu.make_async_copy(index_hbm.at[0, 0], index_slots, slot_sems.at[3])]
    for copy in slots_in:
        copy.start()
    copies = []
    for z in range(CZ):
        copies.append(
            [
                pltpu.make_async_copy(p_hbm.at[z], p_cells.at[z], sems.at[z, 0]),
                pltpu.make_async_copy(sat_hbm.at[0, z], sat_cells.at[0, z], sems.at[z, 1]),
                pltpu.make_async_copy(sat_hbm.at[1, z], sat_cells.at[1, z], sems.at[z, 2]),
            ]
        )
        for copy in copies[-1]:
            copy.start()

    sources = (p_hbm, sat_hbm.at[0], sat_hbm.at[1], k_hbm)
    first_plane = (1 - parity_s[0]) * (CZ - 1)
    planes_in, sides_in = [], []
    for f, source in enumerate(sources):
        for kind, z in ((0, first_plane), (1, CZ - 1 - first_plane)):
            planes_in.append(
                pltpu.make_async_copy(source.at[z], planes.at[kind, f], plane_sems.at[kind, f])
            )
        for side, row in ((0, CX - 8), (1, 0)):
            sides_in.append(
                pltpu.make_async_copy(
                    source.at[:, pl.ds(row, 8), :], edges.at[side, f], edge_sems.at[side, f]
                )
            )
    for copy in planes_in + sides_in:
        copy.start()

    for copy in slots_in:
        copy.wait()
    for half in range(2):
        cols = slice(half * LANES, (half + 1) * LANES)
        here = slice(half * OWNERS, (half + 1) * OWNERS)
        cell = slots[0, :, cols]
        seg = slots[2, :, cols]
        well = lax.shift_right_logical(seg, 1)
        group = lax.shift_right_logical(well * 2731, 16)
        rows_ref[here, :] = (
            (lax.shift_right_logical(cell, 7) & 1) * ROWS
            + slots[1, :, cols] * CX
            + lax.shift_right_logical(cell, 8)
        )
        ints_ref[0, here, :] = cell & (LANES - 1)
        ints_ref[1, here, :] = group
        ints_ref[2, here, :] = well - group * GROUP + (seg & 1) * HALF
        floats_ref[0, here, :] = index_slots[:, cols]
    to_smem.start()

    for z in range(CZ):
        for copy in copies[z]:
            copy.wait()

        def dense(i, carry):
            row = pl.multiple_of(32 * i, 32)
            here = pl.ds(row, 32)
            press = p_cells[z, here, :]
            lam = mobilities(sat_cells[0, z, here, :], sat_cells[1, z, here, :])
            total = lam[0] + lam[1] + lam[2]
            for half in range(2):
                at = pl.ds(pl.multiple_of(half * ROWS + z * CX + row, 32), 32)
                cols = slice(half * LANES, (half + 1) * LANES)
                p_rows[at, :] = press[:, cols]
                m_rows[at, :] = total[:, cols]
            return carry

        lax.fori_loop(0, CX // 32, dense, 0)

    to_smem.wait()
    sub = iota((8, LANES), 0)
    lane = iota((8, LANES), 1)
    places = iota((LANES, LANES), 0)

    def pick(owner, carry):
        for half in range(2):

            @pl.when(blocks_s[0, 0, owner] > half)
            def _():
                block = half * OWNERS + owner
                for group in range(16):
                    grp_p = None
                    grp_m = None
                    for i in range(8):
                        row = rows_s[block, 8 * group + i]
                        row_p = jnp.broadcast_to(p_rows[pl.ds(row, 1), :], (8, LANES))
                        row_m = jnp.broadcast_to(m_rows[pl.ds(row, 1), :], (8, LANES))
                        grp_p = row_p if i == 0 else jnp.where(sub == i, row_p, grp_p)
                        grp_m = row_m if i == 0 else jnp.where(sub == i, row_m, grp_m)
                    p_groups[block, 8 * group : 8 * group + 8, :] = grp_p
                    m_groups[block, 8 * group : 8 * group + 8, :] = grp_m

        return carry

    lax.fori_loop(0, OWNERS, pick, 0)

    for copy in planes_in:
        copy.wait()
    planes_out = [
        pltpu.make_async_copy(planes.at[0], plane_even_hbm, plane_sems.at[0, 0]),
        pltpu.make_async_copy(planes.at[1], plane_odd_hbm, plane_sems.at[1, 0]),
    ]
    for copy in planes_out:
        copy.start()
    for copy in sides_in:
        copy.wait()
    swap = parity_s[1] == 1
    for f in range(4):
        for z in range(CZ):
            last = edges[0, f, z, 7:8, :]
            first = edges[1, f, z, 0:1, :]
            row_even_ref[f, z : z + 1, :] = jnp.where(swap, first, last)
            row_odd_ref[f, z : z + 1, :] = jnp.where(swap, last, first)

    def reduce(step, carry):
        for unit in range(UNROLL):
            owner = step * UNROLL + unit
            count = blocks_s[0, 0, owner]
            values = []
            hots = []
            for half in range(2):
                block = half * OWNERS + owner
                lane_of = jnp.broadcast_to(ints_ref[0, pl.ds(block, 1), :], (8, LANES))
                acc_p = jnp.zeros((8, LANES), F32)
                acc_m = jnp.zeros((8, LANES), F32)
                for group in range(16):
                    keep = lane == 8 * group + sub
                    at = slice(8 * group, 8 * group + 8)
                    grp_p = jnp.take_along_axis(p_groups[block, at, :], lane_of, axis=1)
                    grp_m = jnp.take_along_axis(m_groups[block, at, :], lane_of, axis=1)
                    acc_p = jnp.where(keep, grp_p, acc_p)
                    acc_m = jnp.where(keep, grp_m, acc_m)
                live = count > half
                press = jnp.where(live, jnp.sum(acc_p, axis=0, keepdims=True), 0.0)
                total = jnp.where(live, jnp.sum(acc_m, axis=0, keepdims=True), 0.0)
                floats_ref[1, pl.ds(block, 1), :] = press
                mobile = floats_ref[0, pl.ds(block, 1), :] * total
                group_of = jnp.broadcast_to(ints_ref[1, pl.ds(block, 1), :], (8, LANES)) == sub
                for v in (mobile, mobile * press):
                    values.append(jnp.where(group_of, jnp.broadcast_to(v, (8, LANES)), 0.0))
                spot = jnp.broadcast_to(ints_ref[2, pl.ds(block, 1), :], (LANES, LANES))
                hots += [spot == places, spot == places - 2 * HALF]
            value = jnp.concatenate(values, axis=1)
            high = value.astype(jnp.bfloat16).astype(F32)
            rest = value - high
            middle = rest.astype(jnp.bfloat16).astype(F32)
            low = rest - middle
            pieces = jnp.concatenate([high, middle, low], axis=0).astype(jnp.bfloat16)
            hot = jnp.concatenate(hots, axis=1).astype(F32).astype(jnp.bfloat16)
            out = lax.dot_general(
                pieces, hot, (((1,), (1,)), ((), ())), preferred_element_type=F32
            )
            panel = pl.ds(pl.multiple_of(owner * N_LAYER, 8), N_LAYER)
            sums_ref[panel, :] = out[0:8] + out[8:16] + out[16:24]
        return carry

    lax.fori_loop(0, OWNERS // UNROLL, reduce, 0)
    for copy in planes_out:
        copy.wait()


def gather_sums(blocks, parity, pressure, saturations, permeability, cell, depth, seg, index):
    smem = pl.BlockSpec(memory_space=pltpu.SMEM)
    hbm = pl.BlockSpec(memory_space=pl.ANY)
    vmem = pl.BlockSpec(memory_space=pltpu.VMEM)
    return pl.pallas_call(
        gather_kernel,
        in_specs=[smem, smem] + [hbm] * 7,
        out_specs=[vmem] * 4 + [hbm] * 2 + [vmem] * 2,
        out_shape=[
            jax.ShapeDtypeStruct((DEVICES, LANES), F32),
            jax.ShapeDtypeStruct((2 * OWNERS, LANES), I32),
            jax.ShapeDtypeStruct((3, 2 * OWNERS, LANES), I32),
            jax.ShapeDtypeStruct((2, 2 * OWNERS, LANES), F32),
            pltpu.HBM((4, CX, CY), F32),
            pltpu.HBM((4, CX, CY), F32),
            jax.ShapeDtypeStruct((4, CZ, CY), F32),
            jax.ShapeDtypeStruct((4, CZ, CY), F32),
        ],
        scratch_shapes=[
            pltpu.VMEM((CZ, CX, CY), F32),
            pltpu.VMEM((2, CZ, CX, CY), F32),
            pltpu.VMEM((2 * ROWS, LANES), F32),
            pltpu.VMEM((2 * ROWS, LANES), F32),
            pltpu.VMEM((2 * OWNERS, LANES, LANES), F32),
            pltpu.VMEM((2 * OWNERS, LANES, LANES), F32),
            pltpu.SMEM((2 * OWNERS, LANES), I32),
            pltpu.VMEM((2, 4, CZ, 8, CY), F32),
            pltpu.VMEM((2, 4, CX, CY), F32),
            pltpu.VMEM((3, OWNERS, SLOTS), I32),
            pltpu.VMEM((OWNERS, SLOTS), F32),
            pltpu.SemaphoreType.DMA(()),
            pltpu.SemaphoreType.DMA((CZ, 3)),
            pltpu.SemaphoreType.DMA((2, 4)),
            pltpu.SemaphoreType.DMA((2, 4)),
            pltpu.SemaphoreType.DMA((4,)),
        ],
        compiler_params=pltpu.CompilerParams(vmem_limit_bytes=24 << 20),
        cost_estimate=pl.CostEstimate(flops=0, bytes_accessed=24 << 20, transcendentals=0),
        name="gather_sums",
    )(
        in_hbm(blocks), parity,
        *[in_hbm(v) for v in (pressure, saturations, permeability, cell, depth, seg, index)],
    )


def solve_kernel(sums_ref, parent_ref, cond_ref, target_ref, send_ref, parts):
    total = sums_ref[0:N_LAYER, :]
    for owner in range(1, OWNERS):
        total = total + sums_ref[owner * N_LAYER : (owner + 1) * N_LAYER, :]
    for part in range(4):
        parts[part] = pltpu.roll(total, LANES - HALF * part, 1) if part else total

    ground, load, parent, cond = [], [], [], []
    for s in range(SEG):
        z, k = divmod(s, SEG_SLAB)
        ground.append(parts[k, z : z + 1, :] + RELAX)
        load.append(parts[2 + k, z : z + 1, :] + RELAX * target_ref[s : s + 1, :])
        parent.append(parent_ref[s : s + 1, :])
        cond.append(cond_ref[s : s + 1, :])
    share, own = [None] * SEG, [None] * SEG
    for s in range(SEG - 1, 0, -1):
        inverse = 1.0 / (ground[s] + cond[s])
        share[s] = cond[s] * inverse
        own[s] = load[s] * inverse
        add_ground = share[s] * ground[s]
        add_load = share[s] * load[s]
        for j in range(s):
            hit = parent[s] == j
            ground[j] = ground[j] + jnp.where(hit, add_ground, 0.0)
            load[j] = load[j] + jnp.where(hit, add_load, 0.0)
    value = [load[0] / ground[0]]
    for s in range(1, SEG):
        above = value[0]
        for j in range(1, s):
            above = jnp.where(parent[s] == j, value[j], above)
        value.append(own[s] + share[s] * above)
    for s in range(SEG):
        z, k = divmod(s, SEG_SLAB)
        parts[k, z : z + 1, :] = value[s]
    first = iota((N_LAYER, LANES), 1) < HALF
    panel = jnp.where(first, parts[0], pltpu.roll(parts[1], HALF, 1))
    for owner in range(OWNERS):
        send_ref[owner * N_LAYER : (owner + 1) * N_LAYER, :] = panel


def solve_wells(sums, parent, cond, target):
    vmem = pl.BlockSpec(memory_space=pltpu.VMEM)
    return pl.pallas_call(
        solve_kernel,
        in_specs=[vmem] * 4,
        out_specs=vmem,
        out_shape=jax.ShapeDtypeStruct((DEVICES, LANES), F32),
        scratch_shapes=[pltpu.VMEM((4, N_LAYER, LANES), F32)],
        compiler_params=pltpu.CompilerParams(vmem_limit_bytes=4 << 20),
        cost_estimate=pl.CostEstimate(flops=0, bytes_accessed=1 << 20, transcendentals=0),
        name="solve_wells",
    )(sums, parent, cond, target)


def doubled_mobilities(water, gas_sat):
    oil_sat = 1.0 - water - gas_sat
    return (
        water * water * (2.0 / MU_WATER),
        oil_sat * oil_sat * (2.0 / MU_OIL),
        gas_sat * gas_sat * (2.0 / MU_GAS),
    )


def half_harmonic(left, right):
    return left * right / (left + right)


STRIP = 32


def wide(ref, *index):
    *lead, start, size = index
    return jnp.concatenate(
        [ref[(*lead, pl.ds(half * ROWS + start, size), slice(None))] for half in range(2)], axis=1
    )


def flow_kernel(
    parity_s, p_hbm, sat_hbm, k_hbm, plane_even_ref, plane_odd_ref, row_even_ref, row_odd_ref,
    old_ref, pore_ref, out_ref,
    cells, lams, rolled, zflux, sems
):
    layer = pl.program_id(0)
    now = lax.rem(layer, 2)
    later = 1 - now

    def plane_copies(z):
        sources = (p_hbm.at[z], sat_hbm.at[0, z], sat_hbm.at[1, z], k_hbm.at[z])
        return [
            pltpu.make_async_copy(source, cells.at[f, z], sems.at[z, f])
            for f, source in enumerate(sources)
        ]

    def vertical(low, high):
        trans = GEOMETRY[0] * half_harmonic(low[1], high[1])
        drop = low[0] - high[0]
        flux = []
        for a in range(3):
            potential = drop + GRAVITY[a]
            flux.append(trans * potential * jnp.where(potential > 0, low[2 + a], high[2 + a]))
        return flux

    def level(low, high, mask=None):
        drop = low[0] - high[0]
        rate = half_harmonic(low[1], high[1]) * drop
        if mask is not None:
            rate = jnp.where(mask, 0.0, rate)
        return [rate * jnp.where(drop > 0, low[2 + a], high[2 + a]) for a in range(3)]

    def cell_at(z, row, size):
        rows = pl.ds(row, size)
        return (
            [cells[0, z, rows, :], cells[3, z, rows, :]],
            [cells[1, z, rows, :], cells[2, z, rows, :]],
        )

    def halo_at(from_even, row, size):
        rows = pl.ds(row, size)
        value = [
            jnp.where(from_even, plane_even_ref[f, rows, :], plane_odd_ref[f, rows, :])
            for f in range(4)
        ]
        return [value[0], value[3]], [value[1], value[2]]

    def here_at(row, size):
        rows = pl.ds(row, size)
        return [cells[0, layer, rows, :], cells[3, layer, rows, :]] + [
            lams[now, a, rows, :] for a in range(3)
        ]

    @pl.when(layer == 0)
    def _():
        for z in range(CZ):
            for copy in plane_copies(z):
                copy.start()
        for copy in plane_copies(0):
            copy.wait()

        def first(i, carry):
            row = pl.multiple_of(STRIP * i, STRIP)
            low, low_sat = halo_at(parity_s[0] == 1, row, STRIP)
            high, high_sat = cell_at(0, row, STRIP)
            lam = doubled_mobilities(*high_sat)
            flux = vertical(low + list(doubled_mobilities(*low_sat)), high + list(lam))
            for a in range(3):
                lams[0, a, pl.ds(row, STRIP), :] = lam[a]
                zflux[a, pl.ds(row, STRIP), :] = flux[a]
            return carry

        lax.fori_loop(0, CX // STRIP, first, 0)

    top = iota((8, CY), 0) == 0
    last_lane = iota((STRIP, CY), 1) == CY - 1

    def side_row(from_even):
        here = pl.ds(layer, 1)
        value = [
            jnp.where(from_even, row_even_ref[f, here, :], row_odd_ref[f, here, :])
            for f in range(4)
        ]
        return [value[0], value[3]] + list(doubled_mobilities(value[1], value[2]))

    east = [jnp.broadcast_to(v, (8, CY)) for v in side_row(parity_s[1] == 0)]
    flux = level(side_row(parity_s[1] == 1), [v[0:1] for v in here_at(0, 8)])
    down = tuple(jnp.broadcast_to(f, (8, CY)) for f in flux)
    for f, value in enumerate(here_at(0, STRIP)):
        rolled[f] = pltpu.roll(value, CY - 1, 1)

    def sweep(next_at):
        def step(i, carry):
            row = pl.multiple_of(STRIP * i, STRIP)
            at = pl.ds(row, STRIP)
            final = i == CX // STRIP - 1
            here = here_at(row, STRIP)
            flux_y = level(here, [rolled[f] for f in range(5)], last_lane)
            back_y = [pltpu.roll(f, 1, 1) for f in flux_y]
            after = here_at(
                pl.multiple_of(jnp.minimum(row + STRIP, CX - STRIP), STRIP), STRIP
            )
            after_rolled = [pltpu.roll(v, CY - 1, 1) for v in after]
            neighbour = []
            for v, n, e in zip(here, after, east):
                edge = jnp.where(final, e, n[0:8])
                longer = jnp.concatenate([v, edge], axis=0)
                neighbour.append(pltpu.roll(longer, STRIP + 7, 0)[0:STRIP])
            flux_x = level(here, neighbour)
            down_x = [pltpu.roll(f, 1, 0) for f in flux_x]
            heads = tuple(d[0:8] for d in down_x)
            high, high_sat = next_at(row, STRIP)
            lam = doubled_mobilities(*high_sat)
            flux_z = vertical(here, high + list(lam))
            water = cells[1, layer, at, :]
            gas = cells[2, layer, at, :]
            old_water = old_ref[0, 0, at, :]
            old_gas = old_ref[1, 0, at, :]
            pore = pore_ref[0, at, :]
            change = [
                water - old_water,
                (1.0 - water - gas) - (1.0 - old_water - old_gas),
                gas - old_gas,
            ]
            for a in range(3):
                lams[later, a, at, :] = lam[a]
                net = flux_z[a] - zflux[a, at, :]
                zflux[a, at, :] = flux_z[a]
                before = jnp.concatenate(
                    [jnp.where(top, carry[a], heads[a]), down_x[a][8:]], axis=0
                )
                net = net + (flux_x[a] - before)
                net = net + (flux_y[a] - back_y[a])
                out_ref[a, 0, at, :] = pore * change[a] + net
            for f in range(5):
                rolled[f] = after_rolled[f]
            return heads

        lax.fori_loop(0, CX // STRIP, step, down)

    @pl.when(layer < CZ - 1)
    def _():
        for copy in plane_copies(layer + 1):
            copy.wait()
        sweep(lambda row, size: cell_at(layer + 1, row, size))

    @pl.when(layer == CZ - 1)
    def _():
        sweep(lambda row, size: halo_at(parity_s[0] == 0, row, size))


def cell_flows(parity, pressure, saturations, permeability, planes, sides, old, pore):
    hbm = pl.BlockSpec(memory_space=pl.ANY)
    vmem = pl.BlockSpec(memory_space=pltpu.VMEM)
    return pl.pallas_call(
        flow_kernel,
        grid=(CZ,),
        in_specs=[pl.BlockSpec(memory_space=pltpu.SMEM), hbm, hbm, hbm, vmem, vmem, vmem, vmem]
        + [
            pl.BlockSpec((2, 1, CX, CY), lambda z: (0, z, 0, 0)),
            pl.BlockSpec((1, CX, CY), lambda z: (z, 0, 0)),
        ],
        out_specs=pl.BlockSpec((3, 1, CX, CY), lambda z: (0, z, 0, 0)),
        out_shape=pltpu.HBM((3, CZ, CX, CY), F32),
        scratch_shapes=[
            pltpu.VMEM((4, CZ, CX, CY), F32),
            pltpu.VMEM((2, 3, CX, CY), F32),
            pltpu.VMEM((5, STRIP, CY), F32),
            pltpu.VMEM((3, CX, CY), F32),
            pltpu.SemaphoreType.DMA((CZ, 4)),
        ],
        compiler_params=pltpu.CompilerParams(vmem_limit_bytes=16 << 20),
        cost_estimate=pl.CostEstimate(flops=0, bytes_accessed=20 << 20, transcendentals=0),
        name="cell_flows",
    )(
        parity, in_hbm(pressure), in_hbm(saturations), in_hbm(permeability), *planes, *sides, in_hbm(old), in_hbm(pore)
    )


def inflow_kernel(
    rows_s, blocks_s, areal_s, pw_ref, ints_ref, floats_ref, flow_hbm, sat_hbm,
    out_ref, slab_ref, rate, flows, sats, sems, *sums
):
    layer = pl.program_id(0)

    def layer_copies(z):
        return [
            pltpu.make_async_copy(flow_hbm.at[a, z], flows.at[a, z], sems.at[z, a]) for a in range(3)
        ] + [
            pltpu.make_async_copy(sat_hbm.at[a, z], sats.at[a, z], sems.at[z, 3 + a]) for a in range(2)
        ]

    @pl.when(layer == 0)
    def _():
        for z in range(CZ):
            for copy in layer_copies(z):
                copy.start()
        zero = jnp.zeros((64, LANES), F32)

        def clear(i, carry):
            for acc in sums:
                acc[pl.ds(pl.multiple_of(64 * i, 64), 64), :] = zero
            return carry

        lax.fori_loop(0, 2 * ROWS // 64, clear, 0)
        panels = [pw_ref[pl.ds(g, OWNERS, stride=N_LAYER), :] for g in range(N_LAYER)]
        for half in range(2):
            here = slice(half * OWNERS, (half + 1) * OWNERS)
            group = ints_ref[1, here, :]
            spot = ints_ref[2, here, :]
            well_press = jnp.take_along_axis(panels[0], spot, axis=1)
            for g in range(1, N_LAYER):
                well_press = jnp.where(
                    group == g, jnp.take_along_axis(panels[g], spot, axis=1), well_press
                )
            rate[here, :] = floats_ref[0, here, :] * (floats_ref[1, here, :] - well_press)

        sub = iota((8, LANES), 0)
        lane = iota((8, LANES), 1)

        mine = pw_ref[pl.ds(pl.multiple_of(areal_s[0] * N_LAYER, 8), N_LAYER), :]
        for tile in range(2):
            well = lane + tile * LANES
            group = lax.shift_right_logical(well * 2731, 16)
            for k in range(SEG_SLAB):
                spot = jnp.minimum(well - group * GROUP + k * HALF, LANES - 1)
                value = jnp.where(group == sub, jnp.take_along_axis(mine, spot, axis=1), 0.0)
                value = jnp.sum(value, axis=0, keepdims=True)
                width = min(LANES, WELLS_DEV - tile * LANES)
                slab_ref[k : k + 1, tile * LANES : tile * LANES + width] = value[:, :width]

        def owner_step(owner, carry):
            count = blocks_s[owner]
            for half in range(2):

                @pl.when(count > half)
                def _():
                    block = half * OWNERS + owner
                    lane_of = jnp.broadcast_to(ints_ref[0, pl.ds(block, 1), :], (8, LANES))
                    rate_of = bcast_row(rate, block)
                    for group in range(16):
                        pick = sub + 8 * group
                        place = jnp.take_along_axis(lane_of, pick, axis=1)
                        value = jnp.take_along_axis(rate_of, pick, axis=1)
                        value = jnp.where(lane == place, value, 0.0)
                        for i in range(8):
                            row = rows_s[block, 8 * group + i]
                            acc = sums[i % ACCS]
                            acc[pl.ds(row, 1), :] += value[i : i + 1, :]

            return carry

        lax.fori_loop(0, OWNERS, owner_step, 0)

    for copy in layer_copies(layer):
        copy.wait()

    def combine(i, carry):
        row = pl.multiple_of(32 * i, 32)
        here = pl.ds(row, 32)
        base = pl.multiple_of(layer * CX + row, 8)
        lam = mobilities(sats[0, layer, here, :], sats[1, layer, here, :])
        total = wide(sums[0], base, 32)
        for acc in sums[1:]:
            total = total + wide(acc, base, 32)
        for a in range(3):
            out_ref[a, 0, here, :] = flows[a, layer, here, :] + lam[a] * total
        return carry

    lax.fori_loop(0, CX // 32, combine, 0)


def add_inflow(rows, blocks, areal, pw, ints, floats, flow, saturations):
    hbm = pl.BlockSpec(memory_space=pl.ANY)
    flow_spec = pl.BlockSpec((3, 1, CX, CY), lambda z, *_: (0, z, 0, 0))
    return pl.pallas_call(
        inflow_kernel,
        grid_spec=pltpu.PrefetchScalarGridSpec(
            num_scalar_prefetch=3,
            grid=(CZ,),
            in_specs=[
                pl.BlockSpec((DEVICES, LANES), lambda z, *_: (0, 0)),
                pl.BlockSpec((3, 2 * OWNERS, LANES), lambda z, *_: (0, 0, 0)),
                pl.BlockSpec((2, 2 * OWNERS, LANES), lambda z, *_: (0, 0, 0)),
                hbm,
                hbm,
            ],
            out_specs=[flow_spec, pl.BlockSpec((SEG_SLAB, WELLS_DEV), lambda z, *_: (0, 0))],
            scratch_shapes=[
                pltpu.VMEM((2 * OWNERS, LANES), F32),
                pltpu.VMEM((3, CZ, CX, CY), F32),
                pltpu.VMEM((2, CZ, CX, CY), F32),
                pltpu.SemaphoreType.DMA((CZ, 5)),
            ]
            + [pltpu.VMEM((2 * ROWS, LANES), F32) for _ in range(ACCS)],
        ),
        out_shape=[
            jax.ShapeDtypeStruct((3, CZ, CX, CY), F32),
            jax.ShapeDtypeStruct((SEG_SLAB, WELLS_DEV), F32),
        ],
        compiler_params=pltpu.CompilerParams(vmem_limit_bytes=24 << 20),
        cost_estimate=pl.CostEstimate(flops=0, bytes_accessed=24 << 20, transcendentals=0),
        name="add_inflow",
    )(rows, blocks, areal, pw, ints, floats, in_hbm(flow), in_hbm(saturations))


def on_device(
    pressure,
    saturations,
    old_saturations,
    permeability,
    pore_volume,
    perf_cell,
    perf_layer,
    perf_seg,
    perf_index,
    perf_blocks,
    seg_parent,
    seg_cond,
    seg_target,
):
    n_areal = lax.axis_size("areal")
    n_layer = lax.axis_size("layer")
    layer = lax.axis_index("layer").astype(I32)
    areal = lax.axis_index("areal").astype(I32).reshape(1)
    blocks = perf_blocks[0, 0]
    parity = jnp.concatenate([layer.reshape(1), areal]) & 1

    def own_wells(values):
        part = lax.dynamic_slice_in_dim(values, layer * GROUP, GROUP, axis=0)
        return jnp.pad(part.T, ((0, 0), (0, LANES - GROUP)))

    def even_swap(values, axis, count):
        return lax.ppermute(values, axis, [(i, i ^ 1) for i in range(count)])

    def odd_swap(values, axis, count):
        pairs = [(i, i + 1) for i in range(1, count - 1, 2)]
        return lax.ppermute(values, axis, pairs + [(j, i) for i, j in pairs])

    def exchange(values):
        return lax.all_to_all(values, ("areal", "layer"), split_axis=0, concat_axis=0, tiled=True)

    sums, rows, ints, floats, *packed = gather_sums(
        perf_blocks, parity, pressure, saturations, permeability,
        perf_cell, perf_layer, perf_seg, perf_index,
    )
    received = exchange(sums)
    plane_even = even_swap(packed[0], "layer", n_layer)
    plane_odd = odd_swap(packed[1], "layer", n_layer)
    row_even = even_swap(packed[2], "areal", n_areal)
    row_odd = odd_swap(packed[3], "areal", n_areal)
    planes, sides = (plane_even, plane_odd), (row_even, row_odd)
    systems = [own_wells(v) for v in (seg_parent, seg_cond, seg_target)]
    solved = solve_wells(received, *systems)
    pw = exchange(solved)
    flow = cell_flows(
        parity, pressure, saturations, permeability, planes, sides, old_saturations, pore_volume
    )
    residual, slab = add_inflow(
        rows, blocks, areal, pw, ints, floats, flow, saturations
    )
    return residual, slab.T


def solution(mesh):
    return jax.shard_map(
        on_device,
        mesh=mesh,
        in_specs=(
            P("layer", "areal", None),
            P(None, "layer", "areal", None),
            P(None, "layer", "areal", None),
            P("layer", "areal", None),
            P("layer", "areal", None),
            P("layer", "areal", None, None),
            P("layer", "areal", None, None),
            P("layer", "areal", None, None),
            P("layer", "areal", None, None),
            P("layer", "areal", None),
            P("areal", None),
            P("areal", None),
            P("areal", None),
        ),
        out_specs=(P(None, "layer", "areal", None), P("areal", "layer")),
        check_vma=False,
    )
```
